32 devices in a mesh: shots: 2 (over x), depth: 8 (over z, y), freq: 2 (over core).
Axes of the slice: x: 2, y: 2, z: 4, core: 2. Of those that a mesh axis runs over, the one named last changes fastest.
Arguments:
- surface: float32 [2, 4, 2, 128, 256], P('shots', 'freq'), parts along dimension 0, may hold values from -2.1 to 2.1
- bins: int32 [8, 128, 128], P('depth'), may hold values from 0 to 7
- stencil: float32 [4, 8, 5], P('freq'), may hold values from 0.25 to 1
- phase_step: float32 [4, 8], P('freq'), may hold values from 0.3 to 1.4
- phase_shift: float32 [4, 8], P('freq'), may hold values from -3.140625 to 3.140625
- lags: int32 [4], replicated, may hold values from 0 to 7, as said below
Outputs:
- image: float32 [8, 8, 16384], P('depth', 'shots', 'freq'), parts along dimension 1
The draws below stay inside these ranges and needn't reach their ends.
There are 2 independent parts, one for each index of `shots`. The reference program is written for one: setup_inputs(seed, part) draws one part's arguments, and reference() takes and returns one part's arrays. A program takes and returns all parts, laid end to end along the dimension named above; an argument that names none is the same for every part. Nothing has to cross between parts.
Inputs may be any that keep to these rules, and one draw needn't show every extreme that they name: `lags`: 4 distinct half-offsets in cells; one of them is 7.
All inputs are finite; a program needn't handle non-finite values.
Results may differ from the reference program's by a relative error of at most 0.0003.
Values sent between devices are 32-bit elements; how exact they have to be, the bound alone decides.
No kernel may reach another device: no remote copies, remote signals or barrier semaphores. Data moves between devices by JAX's collectives and lax.ppermute only.
A program may use at most 64 MiB of HBM per device.

```python
import math
import jax
import jax.numpy as jnp
from jax import lax

G = 128
SHOTS = 1
KERNELS = 8
TAPS = 13
HALF = 6
LAGS = 4
HMAX = 7
NF = 4
NZ = 8


def draw_lags(key, part):
    order = jax.random.permutation(key, HMAX).astype(jnp.int32)
    chosen = jnp.concatenate([order[:LAGS - 1], jnp.array([HMAX], jnp.int32)])
    return jax.random.permutation(jax.random.fold_in(key, 7), chosen).astype(jnp.int32)


def plant(result, stream_key, low, largest):
    shape = result.shape
    spot = [jax.random.randint(jax.random.fold_in(stream_key, axis), (), 0, shape[axis]) for axis in range(len(shape))]
    result = result.at[tuple(spot)].set(low)
    longest = shape.index(max(shape))
    spot[longest] = (spot[longest] + 1) % shape[longest]
    return result.at[tuple(spot)].set(largest)


def block_scale(own_key, extent, pieces, smallest, high):
    def one(position, blocks):
        steps = jax.random.uniform(jax.random.fold_in(jax.random.fold_in(own_key, 6), position), (blocks,), jnp.float32, smallest / len(pieces), high / len(pieces))
        return jnp.repeat(jnp.exp(steps), extent[position] // blocks).reshape((-1,) + (1,) * (len(extent) - position - 1))

    gain = one(*pieces[0])
    for cut in pieces[1:]:
        gain = gain * one(*cut)
    return gain


def bell_draw(key, shape, deviation, most, split=(), kind=jnp.bfloat16):
    entries = deviation * jax.random.normal(key, shape, jnp.float32)
    if split:
        entries = entries * block_scale(key, shape, split, -0.22, 0.18)
    return jnp.clip(entries, -most, most).astype(kind)


def setup_inputs(seed: int = 0, part: int = 0) -> dict:
    key_of = jax.random.split(jax.random.key(seed), 7)
    part_keys = jax.random.split(jax.random.fold_in(key_of[6], part), 7)
    surface = bell_draw(part_keys[0], (SHOTS, NF, 2, G, 2 * G), 0.35, 2.1, ((1, 2),), jnp.float32)
    bins = plant(jax.random.randint(key_of[1], (NZ, G, G), 0, KERNELS), jax.random.fold_in(key_of[1], 1), 0, KERNELS - 1).astype(jnp.int32)
    stencil = jnp.clip(0.25 + 0.75 * jax.random.uniform(key_of[2], (NF, KERNELS, 5), jnp.float32) ** block_scale(key_of[2], (NF, KERNELS, 5), ((0, 2),), -0.2, 0.2), 0.25, 1.0)
    phase_step = jnp.clip(jnp.exp(math.log(1.4) - 1.540445 * jax.random.uniform(key_of[3], (NF, KERNELS), jnp.float32) ** block_scale(key_of[3], (NF, KERNELS), ((0, 2),), -0.2, 0.2)), 0.3, 1.4)
    phase_shift = jnp.clip(jax.random.uniform(key_of[4], (NF, KERNELS), jnp.float32, -3.140625, 3.140625), -3.140625, 3.140625)
    lags = draw_lags(jax.random.fold_in(key_of[6], 71), part)
    return dict(surface=surface, bins=bins, stencil=stencil, phase_step=phase_step, phase_shift=phase_shift, lags=lags)


def kernel_taps(stencil, phase_step, phase_shift):
    center = stencil[..., 0]
    along_x = stencil[..., 1]
    along_y = stencil[..., 2]
    diag_main = stencil[..., 3]
    diag_anti = stencil[..., 4]
    row_above = jnp.stack([diag_main, along_y, diag_anti], -1)
    row_middle = jnp.stack([along_x, center, along_x], -1)
    row_below = jnp.stack([diag_anti, along_y, diag_main], -1)
    stencil_grid = jnp.stack([row_above, row_middle, row_below], -2)
    weight_sum = center + 2.0 * (along_x + along_y + diag_main + diag_anti)
    stencil_grid = stencil_grid * (phase_step / weight_sum)[..., None, None]
    lead = stencil.shape[:-1]
    tap_rows = lax.broadcasted_iota(jnp.int32, (TAPS, TAPS), 0)
    tap_cols = lax.broadcasted_iota(jnp.int32, (TAPS, TAPS), 1)
    unit_tap = ((tap_rows == HALF) & (tap_cols == HALF)).astype(jnp.float32)
    power = jnp.broadcast_to(unit_tap, lead + (TAPS, TAPS)).astype(jnp.float32)
    real_sum = power
    imag_sum = jnp.zeros(lead + (TAPS, TAPS), jnp.float32)
    pad_spec = [(0, 0)] * len(lead) + [(1, 1), (1, 1)]
    for order in range(1, HALF + 1):
        padded = jnp.pad(power, pad_spec)
        grown = jnp.zeros(lead + (TAPS, TAPS), jnp.float32)
        for row_off in range(3):
            for col_off in range(3):
                piece = padded[..., 2 - row_off:2 - row_off + TAPS, 2 - col_off:2 - col_off + TAPS]
                grown = grown + stencil_grid[..., row_off, col_off, None, None] * piece
        power = grown
        weighted = power * (1.0 / math.factorial(order))
        if order % 4 == 1:
            imag_sum = imag_sum + weighted
        elif order % 4 == 2:
            real_sum = real_sum - weighted
        elif order % 4 == 3:
            imag_sum = imag_sum - weighted
        else:
            real_sum = real_sum + weighted
    cosine = jnp.cos(phase_shift)[..., None, None]
    sine = jnp.sin(phase_shift)[..., None, None]
    return cosine * real_sum - sine * imag_sum, sine * real_sum + cosine * imag_sum


def reference(surface, bins, stencil, phase_step, phase_shift, lags):
    kern_real, kern_imag = kernel_taps(stencil, phase_step, phase_shift)
    padded_size = G + 2 * HALF
    kernel = kern_real + 1j * kern_imag
    flipped = kernel[..., ::-1, ::-1]
    placed = jnp.pad(flipped, ((0, 0), (0, 0), (0, padded_size - TAPS), (0, padded_size - TAPS)))
    placed = jnp.roll(placed, (-HALF, -HALF), axis=(2, 3))
    spectrum = jnp.fft.fft2(placed)
    wavefield = surface[..., :G] + 1j * surface[..., G:]
    kernel_ids = jnp.arange(KERNELS).astype(jnp.int32)

    def descend(fields, level_bins):
        padded = jnp.pad(fields, ((0, 0), (0, 0), (0, 0), (0, padded_size - G), (0, padded_size - G)))
        field_spec = jnp.fft.fft2(padded)
        convolved = jnp.fft.ifft2(field_spec[:, :, :, None] * spectrum[None, :, None])[..., :G, :G]
        selector = (level_bins[None] == kernel_ids[:, None, None]).astype(jnp.float32)
        fields = jnp.sum(convolved * selector, axis=3)
        source_pad = jnp.pad(fields[:, :, 0], ((0, 0), (0, 0), (0, 0), (HMAX, HMAX)))
        receiver_pad = jnp.pad(fields[:, :, 1], ((0, 0), (0, 0), (0, 0), (HMAX, HMAX)))
        lag_terms = []
        for lag_index in range(LAGS):
            offset = lags[lag_index].astype(jnp.int32)
            shifted_source = lax.dynamic_slice_in_dim(source_pad, (HMAX - offset).astype(jnp.int32), G, 3)
            shifted_receiver = lax.dynamic_slice_in_dim(receiver_pad, (HMAX + offset).astype(jnp.int32), G, 3)
            product = jnp.real(jnp.conj(shifted_source) * shifted_receiver)
            lag_terms.append(jnp.sum(product, axis=(0, 1)).reshape(G * G))
        return fields, jnp.stack(lag_terms)

    unused, image = lax.scan(descend, wavefield, bins)
    return image
```

```python
import functools
import math

import jax
import jax.numpy as jnp
from jax import lax
from jax.experimental import pallas as pl
from jax.experimental.pallas import tpu as pltpu
from jax.sharding import PartitionSpec as P

KERNELS = 8
LAGS = 4
HMAX = 7

TAPS = 13
HALF = 6
TILE = 16
WIN = 32
LANES = 128
BF = jnp.bfloat16
F32 = jnp.float32


def column(row):
    n = row.shape[1]
    eye = lax.broadcasted_iota(jnp.int32, (n, n), 0) == lax.broadcasted_iota(jnp.int32, (n, n), 1)
    return jnp.sum(jnp.where(eye, jnp.broadcast_to(row, (n, n)), 0.0), axis=1, keepdims=True)


def lane_taps(stencil, step, shift):
    kernels = stencil.shape[0]
    lanes = 512
    weight = [stencil[:, i : i + 1] for i in range(5)]
    total = weight[0] + 2.0 * (weight[1] + weight[2] + weight[3] + weight[4])
    scale = step / total
    weight = [w * scale for w in weight]
    lane = lax.broadcasted_iota(jnp.int32, (kernels, lanes), 1)
    power = (lane == HALF * WIN + HALF).astype(F32)
    real, imag = power, jnp.zeros((kernels, lanes), F32)

    def both(value, distance):
        return pltpu.roll(value, distance, 1) + pltpu.roll(value, lanes - distance, 1)

    for order in range(1, HALF + 1):
        power = (
            weight[0] * power
            + weight[1] * both(power, WIN)
            + weight[2] * both(power, 1)
            + weight[3] * both(power, WIN + 1)
            + weight[4] * both(power, WIN - 1)
        )
        term = power * (1.0 / math.factorial(order))
        if order % 4 == 1:
            imag = imag + term
        elif order % 4 == 2:
            real = real - term
        elif order % 4 == 3:
            imag = imag - term
        else:
            real = real + term
    cosine, sine = jnp.cos(shift), jnp.sin(shift)
    return cosine * real - sine * imag, sine * real + cosine * imag


def split(value):
    high = value.astype(BF)
    return high, (value - high.astype(F32)).astype(BF)


def levels_kernel(dims, place, lags, surface, bins, stencil, step, shift, image,
                  weights, wide, grid_pad, bins_pad, high, low, state):
    levels, kernels, strip, grid, lag_count = dims
    halo = HALF * levels
    freq, first = place[0], place[1]
    real, imag = lane_taps(stencil[freq], column(step[pl.ds(freq, 1), :]), column(shift[pl.ds(freq, 1), :]))
    for which, taps in enumerate((real, real + imag, imag - real)):
        for row in range(TILE):
            moved = pltpu.roll(taps, row, 1) if row else taps
            for chunk in range(4):
                wide[chunk, pl.ds(row, kernels, stride=TILE), :] = moved[:, chunk * LANES : (chunk + 1) * LANES]
        for chunk in range(4):
            w_high, w_low = split(wide[chunk])
            weights[which, : kernels * TILE, chunk * LANES : (chunk + 1) * LANES] = w_high
            weights[which, kernels * TILE :, chunk * LANES : (chunk + 1) * LANES] = w_low
    bins_pad[...] = jnp.full(bins_pad.shape, kernels, jnp.int32)
    for slot in range(levels):
        bins_pad[lax.rem(place[2] - slot + levels, levels), halo : halo + grid, :] = bins[slot]
    grid_pad[...] = jnp.zeros(grid_pad.shape, F32)
    for field in range(2):
        for part in range(2):
            grid_pad[2 * field + part, halo : halo + grid, :] = surface[freq, field, :, part * LANES : (part + 1) * LANES]
    lane = lax.broadcasted_iota(jnp.int32, (TILE, LANES), 1)

    def spread(slot, row, planes):
        for tap in range(TAPS):
            reach = tap - HALF
            moved = []
            for plane in planes:
                if reach:
                    plane = pltpu.roll(plane, (-reach) % LANES, 1)
                    inside = lane < LANES - reach if reach > 0 else lane >= -reach
                    plane = jnp.where(inside, plane, 0.0)
                moved.append(plane)
            for field in range(2):
                re, im = moved[2 * field], moved[2 * field + 1]
                for which, value in enumerate((re + im, im, re)):
                    v_high, v_low = split(value)
                    high[slot, which, tap, pl.ds(row, TILE), field * LANES : (field + 1) * LANES] = v_high
                    low[slot, which, tap, pl.ds(row, TILE), field * LANES : (field + 1) * LANES] = v_low

    base = first + halo - halo

    def fill(index, carry):
        row = pl.multiple_of(index * TILE, TILE)
        spread(0, row, [grid_pad[plane, pl.ds(base + row, TILE), :] for plane in range(4)])
        return carry

    most = strip + 2 * halo
    lax.fori_loop(0, (most - 2 * HALF + TILE - 1) // TILE + 1, fill, 0)

    def level(index, carry):
        slot = index % 2
        needed = strip + 2 * HALF * (levels - 1 - index)
        bins_base = base + HALF * (index + 1)

        def tile(number, inner):
            row = pl.multiple_of(number * TILE, TILE)
            cell_bins = bins_pad[index, pl.ds(bins_base + row, TILE), :]
            sums = []
            for which in range(3):
                rhs = high[slot, which, :, pl.ds(row, WIN), :].reshape(TAPS * WIN, 2 * LANES)
                rhs_low = low[slot, which, :, pl.ds(row, WIN), :].reshape(TAPS * WIN, 2 * LANES)
                out = jnp.dot(weights[which, :, : TAPS * WIN], rhs, preferred_element_type=F32)
                out_low = jnp.dot(weights[which, : kernels * TILE, : TAPS * WIN], rhs_low, preferred_element_type=F32)
                out = out[: kernels * TILE] + out[kernels * TILE :] + out_low
                for field in range(2):
                    chosen = jnp.zeros((TILE, LANES), F32)
                    for k in range(kernels):
                        chosen = jnp.where(cell_bins == k, out[k * TILE : (k + 1) * TILE, field * LANES : (field + 1) * LANES], chosen)
                    sums.append(chosen)
            planes = []
            for field in range(2):
                planes.append(sums[field] - sums[2 + field])
                planes.append(sums[field] + sums[4 + field])
            for plane in range(4):
                state[plane, pl.ds(row, TILE), :] = planes[plane]
            spread(1 - slot, row, planes)
            return inner

        lax.fori_loop(0, (needed + TILE - 1) // TILE, tile, 0)
        start = halo - HALF * (index + 1)
        planes = [state[plane, pl.ds(start, strip), :] for plane in range(4)]
        lanes = lax.broadcasted_iota(jnp.int32, (strip, LANES), 1)
        for number in range(lag_count):
            offset = lags[number]
            away = lax.rem(LANES - offset, LANES)
            s_re, s_im = pltpu.roll(planes[0], offset, 1), pltpu.roll(planes[1], offset, 1)
            r_re, r_im = pltpu.roll(planes[2], away, 1), pltpu.roll(planes[3], away, 1)
            inside = (lanes >= offset) & (lanes < LANES - offset)
            image[index, number] = jnp.where(inside, s_re * r_re + s_im * r_im, 0.0)
        return carry

    lax.fori_loop(0, levels, level, 0)


def run_levels(place, lags, surface, bins, stencil, step, shift, strip):
    freqs, _, grid, _ = surface.shape
    levels = bins.shape[0]
    kernels = stencil.shape[1]
    halo = HALF * levels
    most = strip + 2 * halo
    tiles = (most - 2 * HALF + TILE - 1) // TILE
    rows = (tiles + 1) * TILE
    padded = grid - strip + rows
    padded = (padded + 7) // 8 * 8
    padded = max(padded, halo + grid)
    dims = (levels, kernels, strip, grid, lags.shape[0])
    vm = pl.BlockSpec(memory_space=pltpu.VMEM)
    sm = pl.BlockSpec(memory_space=pltpu.SMEM)
    return pl.pallas_call(
        functools.partial(levels_kernel, dims),
        out_shape=jax.ShapeDtypeStruct((levels, lags.shape[0], strip, grid), F32),
        in_specs=[sm, sm, vm, vm, vm, vm, vm],
        out_specs=vm,
        scratch_shapes=[
            pltpu.VMEM((3, 2 * kernels * TILE, 512), BF),
            pltpu.VMEM((4, kernels * TILE, LANES), F32),
            pltpu.VMEM((4, padded, LANES), F32),
            pltpu.VMEM((levels, padded, LANES), jnp.int32),
            pltpu.VMEM((2, 3, TAPS, rows, 2 * LANES), BF),
            pltpu.VMEM((2, 3, TAPS, rows, 2 * LANES), BF),
            pltpu.VMEM((4, rows, LANES), F32),
        ],
        compiler_params=pltpu.CompilerParams(vmem_limit_bytes=60 * 1024 * 1024),
    )(place, lags, surface, bins, stencil, step, shift)


column_tile = 16


def from_behind(value, axis, steps):
    count = lax.axis_size(axis)
    initial, last = (max(0, -steps), min(count, count - steps))
    return lax.ppermute(value, axis, [(source, source + steps) for source in range(initial, last)])


def kernel_taps(stencil, phase_step, phase_shift):
    center = stencil[..., 0]
    along_x = stencil[..., 1]
    along_y = stencil[..., 2]
    diag_main = stencil[..., 3]
    diag_anti = stencil[..., 4]
    row_above = jnp.stack([diag_main, along_y, diag_anti], -1)
    row_middle = jnp.stack([along_x, center, along_x], -1)
    row_below = jnp.stack([diag_anti, along_y, diag_main], -1)
    stencil_grid = jnp.stack([row_above, row_middle, row_below], -2)
    weight_sum = center + 2.0 * (along_x + along_y + diag_main + diag_anti)
    stencil_grid = stencil_grid * (phase_step / weight_sum)[..., None, None]
    lead = stencil.shape[:-1]
    tap_rows = lax.broadcasted_iota(jnp.int32, (TAPS, TAPS), 0)
    tap_cols = lax.broadcasted_iota(jnp.int32, (TAPS, TAPS), 1)
    unit_tap = ((tap_rows == HALF) & (tap_cols == HALF)).astype(jnp.float32)
    power = jnp.broadcast_to(unit_tap, lead + (TAPS, TAPS))
    real_sum = power
    imag_sum = jnp.zeros(lead + (TAPS, TAPS), jnp.float32)
    pad_spec = [(0, 0)] * len(lead) + [(1, 1), (1, 1)]
    for order in range(1, HALF + 1):
        padded = jnp.pad(power, pad_spec)
        grown = jnp.zeros(lead + (TAPS, TAPS), jnp.float32)
        for row_off in range(3):
            for col_off in range(3):
                piece = padded[
                    ..., 2 - row_off : 2 - row_off + TAPS, 2 - col_off : 2 - col_off + TAPS
                ]
                grown = grown + stencil_grid[..., row_off, col_off, None, None] * piece
        power = grown
        weighted = power * (1.0 / math.factorial(order))
        if order % 4 == 1:
            imag_sum = imag_sum + weighted
        elif order % 4 == 2:
            real_sum = real_sum - weighted
        elif order % 4 == 3:
            imag_sum = imag_sum - weighted
        else:
            real_sum = real_sum + weighted
    cosine = jnp.cos(phase_shift)[..., None, None]
    sine = jnp.sin(phase_shift)[..., None, None]
    return (cosine * real_sum - sine * imag_sum, sine * real_sum + cosine * imag_sum)


def advance_level(fields, weights, selector):
    field_count = fields.shape[0]
    grid_width = fields.shape[1]
    tiles = grid_width // column_tile
    parts = fields.reshape(field_count, grid_width, 2, grid_width)
    padded = jnp.pad(parts, ((0, 0), (HALF, HALF), (0, 0), (HALF, column_tile - HALF)))
    main = padded[..., :grid_width].reshape(
        field_count, grid_width + 2 * HALF, 2, tiles, column_tile
    )
    after = padded[..., column_tile : grid_width + column_tile].reshape(
        field_count, grid_width + 2 * HALF, 2, tiles, column_tile
    )
    windows = jnp.concatenate([main, after[..., : 2 * HALF]], -1)
    windows = jnp.transpose(windows, (0, 1, 3, 2, 4))
    patches = jnp.stack(
        [windows[:, row_tap : row_tap + grid_width] for row_tap in range(TAPS)], axis=3
    )
    patches = patches.reshape(field_count * grid_width * tiles, TAPS * 2 * (column_tile + 2 * HALF))
    result = jnp.dot(
        patches, weights, precision=lax.Precision.HIGHEST, preferred_element_type=jnp.float32
    )
    result = result.reshape(field_count, grid_width, tiles, KERNELS, 2, column_tile)
    chosen = jnp.sum(result * selector[None], axis=3)
    return jnp.transpose(chosen, (0, 1, 3, 2, 4)).reshape(field_count, grid_width, 2 * grid_width)


def image_terms(source, receiver, lags):
    grid_width = source.shape[0]
    source_parts = jnp.pad(
        source.reshape(grid_width, 2, grid_width), ((0, 0), (0, 0), (HMAX, HMAX))
    )
    receiver_parts = jnp.pad(
        receiver.reshape(grid_width, 2, grid_width), ((0, 0), (0, 0), (HMAX, HMAX))
    )
    lag_terms = []
    for lag_index in range(LAGS):
        offset = lags[lag_index]
        shifted_source = lax.dynamic_slice_in_dim(source_parts, HMAX - offset, grid_width, 2)
        shifted_receiver = lax.dynamic_slice_in_dim(receiver_parts, HMAX + offset, grid_width, 2)
        lag_terms.append(jnp.sum(shifted_source * shifted_receiver, axis=1))
    return jnp.stack(lag_terms)


def pipeline_body(surface, bins, stencil, phase_step, phase_shift, lags):
    shot_count = surface.shape[0]
    freq_count = surface.shape[1]
    grid_width = surface.shape[3]
    slab_steps = bins.shape[0]
    tiles = grid_width // column_tile
    window_width = column_tile + 2 * HALF
    depth_count = lax.axis_size("depth")
    depth_index = lax.axis_index("depth")
    kern_real, kern_imag = kernel_taps(stencil, phase_step, phase_shift)
    mixing = jnp.stack(
        [jnp.stack([kern_real, kern_imag], 1), jnp.stack([-kern_imag, kern_real], 1)], 1
    )
    window_ids = lax.broadcasted_iota(jnp.int32, (window_width, column_tile, TAPS), 0)
    out_ids = lax.broadcasted_iota(jnp.int32, (window_width, column_tile, TAPS), 1)
    tap_ids = lax.broadcasted_iota(jnp.int32, (window_width, column_tile, TAPS), 2)
    shift_table = (window_ids == out_ids + tap_ids).astype(jnp.float32)
    all_weights = jnp.einsum(
        "fpqkab,cwb->fapckqw", mixing, shift_table, precision=lax.Precision.HIGHEST
    )
    all_weights = all_weights.reshape(
        freq_count, TAPS * 2 * window_width, KERNELS * 2 * column_tile
    )
    kernel_ids = lax.broadcasted_iota(jnp.int32, (1, 1, 1, KERNELS, 1, 1), 3)
    selectors = (
        bins.reshape(slab_steps, grid_width, tiles, 1, 1, column_tile) == kernel_ids
    ).astype(jnp.float32)
    image_part = jnp.zeros((slab_steps, LAGS, grid_width, grid_width), jnp.float32)
    front_count = shot_count * freq_count

    def advance_turn(step_index, carry):
        sent, image_now = carry
        received = from_behind(sent, "depth", 1)
        front_index = step_index - depth_index
        active = (front_index >= 0) & (front_index < front_count)
        clipped = jnp.clip(front_index, 0, front_count - 1)
        shot_index = clipped // freq_count
        freq_index = clipped % freq_count
        shot_fields = lax.dynamic_index_in_dim(surface, shot_index, 0, keepdims=False)
        surface_front = lax.dynamic_index_in_dim(shot_fields, freq_index, 0, keepdims=False)
        incoming = jnp.where(depth_index == 0, surface_front, received)
        weights_front = lax.dynamic_index_in_dim(all_weights, freq_index, 0, keepdims=False)

        def compute_front(state):
            fields, image_held = state
            fields = advance_level(fields, weights_front, selectors[0])
            level_terms = [image_terms(fields[0], fields[1], lags)]
            return (fields, image_held + jnp.stack(level_terms))

        def keep_state(state):
            return state

        return lax.cond(active, compute_front, keep_state, (incoming, image_now))

    start = (jnp.zeros((2, grid_width, 2 * grid_width), jnp.float32), image_part)
    final_sent, image_part = lax.fori_loop(0, depth_count + front_count - 1, advance_turn, start)
    image_part = image_part.reshape(slab_steps, LAGS, grid_width * grid_width)
    return lax.psum_scatter(image_part, "freq", scatter_dimension=2, tiled=True)


def gather_bins(bins):
    count, cores = lax.axis_size("depth"), lax.axis_size("freq")
    core = lax.axis_index("freq")
    rounds = -(-(count - 1) // cores)
    received = []
    for number in range(rounds):
        pairs = []
        for own in range(cores):
            turn = 1 + number + own * rounds
            if turn < count:
                pairs += [(place * cores + own, (place + turn) % count * cores + own) for place in range(count)]
        received.append(lax.ppermute(bins[0], ("depth", "freq"), pairs))
    mine = jnp.stack(received)
    theirs = lax.ppermute(mine, "freq", [(0, 1), (1, 0)])
    first = jnp.where(core == 0, mine, theirs)
    second = jnp.where(core == 0, theirs, mine)
    return jnp.concatenate([bins, first, second])[:count]


def spread_image(image, freqs):
    count, cores = lax.axis_size("depth"), lax.axis_size("freq")
    depth, core = lax.axis_index("depth"), lax.axis_index("freq")
    strips = count // freqs
    half = strips // cores
    levels, lags, strip, grid = image.shape
    block = image.reshape(half, cores, freqs, lags, strip, grid)
    kept = lax.dynamic_index_in_dim(block, core, 1, keepdims=False)
    given = lax.dynamic_index_in_dim(block, 1 - core, 1, keepdims=False)
    block = kept + lax.ppermute(given, "freq", [(0, 1), (1, 0)])
    place = depth % freqs
    kept = lax.dynamic_index_in_dim(block, place, 1, keepdims=False)
    given = lax.dynamic_index_in_dim(block, 1 - place, 1, keepdims=False)
    block = kept + lax.ppermute(given, "depth", [(d, d ^ 1) for d in range(count)])
    mine = depth // freqs
    parts = []
    for number in range(half):
        pairs = []
        for z in range(strips):
            for y in range(freqs):
                for c in range(cores):
                    target = c + cores * ((z % half + number) % half)
                    pairs.append(((z * freqs + y) * cores + c, (target * freqs + y) * cores + z // half))
        chunk = lax.dynamic_index_in_dim(block, (mine % half + number) % half, 0, keepdims=False)
        parts.append(lax.ppermute(chunk, ("depth", "freq"), pairs))
    stacked = jnp.stack(parts)
    row = mine // cores
    ordered = jnp.stack([lax.dynamic_index_in_dim(stacked, (row - r) % half, 0, keepdims=False) for r in range(half)], 1)
    return ordered.reshape(1, lags, half * strip * grid)


def strip_body(surface, bins, stencil, phase_step, phase_shift, lags):
    freqs, grid = surface.shape[1], surface.shape[3]
    depth = lax.axis_index("depth")
    strip = grid * freqs // lax.axis_size("depth")
    place = jnp.stack([depth % freqs, depth // freqs * strip, depth]).astype(jnp.int32)
    image = run_levels(place, lags, surface[0], gather_bins(bins), stencil, phase_step, phase_shift, strip)
    return spread_image(image, freqs)


def body(surface, bins, stencil, phase_step, phase_shift, lags):
    count, cores = lax.axis_size("depth"), lax.axis_size("freq")
    freqs, grid = surface.shape[1], surface.shape[3]
    strips = count // freqs
    fits = (
        surface.shape[0] == 1
        and bins.shape[0] == 1
        and grid == LANES
        and cores == 2
        and freqs == 2
        and count % freqs == 0
        and strips % cores == 0
        and grid % strips == 0
        and (grid // strips) % 8 == 0
        and HALF * count <= grid // 2
    )
    way = strip_body if fits else pipeline_body
    return way(surface, bins, stencil, phase_step, phase_shift, lags)


def solution(mesh):
    return jax.shard_map(
        body,
        mesh=mesh,
        in_specs=(
            P("shots", "freq", None, None, None),
            P("depth", None, None),
            P("freq", None, None),
            P("freq", None),
            P("freq", None),
            P(),
        ),
        out_specs=P("depth", "shots", "freq"),
        check_vma=False,
    )
```

```python
import functools
import math

import jax
import jax.numpy as jnp
from jax import lax
from jax.experimental import pallas as pl
from jax.experimental.pallas import tpu as pltpu
from jax.sharding import PartitionSpec as P

KERNELS = 8
LAGS = 4
HMAX = 7
TAPS = 13
HALF = 6
TILE = 16
WIN = 32
LANES = 128
BF = jnp.bfloat16
F32 = jnp.float32


def column(row):
    n = row.shape[1]
    eye = lax.broadcasted_iota(jnp.int32, (n, n), 0) == lax.broadcasted_iota(jnp.int32, (n, n), 1)
    return jnp.sum(jnp.where(eye, jnp.broadcast_to(row, (n, n)), 0.0), axis=1, keepdims=True)


def lane_taps(weight, step, shift):
    kernels = step.shape[0]
    lanes = 512
    total = weight[0] + 2.0 * (weight[1] + weight[2] + weight[3] + weight[4])
    scale = step / total
    weight = [w * scale for w in weight]
    lane = lax.broadcasted_iota(jnp.int32, (kernels, lanes), 1)
    power = (lane == HALF * WIN + HALF).astype(F32)
    real, imag = power, jnp.zeros((kernels, lanes), F32)

    def both(value, distance):
        return pltpu.roll(value, distance, 1) + pltpu.roll(value, lanes - distance, 1)

    for order in range(1, HALF + 1):
        power = (
            weight[0] * power
            + weight[1] * both(power, WIN)
            + weight[2] * both(power, 1)
            + weight[3] * both(power, WIN + 1)
            + weight[4] * both(power, WIN - 1)
        )
        term = power * (1.0 / math.factorial(order))
        if order % 4 == 1:
            imag = imag + term
        elif order % 4 == 2:
            real = real - term
        elif order % 4 == 3:
            imag = imag - term
        else:
            real = real + term
    cosine, sine = jnp.cos(shift), jnp.sin(shift)
    return cosine * real - sine * imag, sine * real + cosine * imag


def split(value):
    high = value.astype(BF)
    return high, (value - high.astype(F32)).astype(BF)


def tile_counts(levels, strip):
    return [-(-(strip + 2 * HALF * (levels - 1 - level)) // TILE) for level in range(levels)]


def levels_kernel(dims, lags, surface, own, mine, theirs, stencil, step, shift, image,
                  weights, wide, grid_pad, bins_pad, high0, low0, high1, low1, state):
    levels, kernels, freqs, strip, grid, lag_count = dims
    halo = HALF * levels
    depth, core = lax.axis_index("depth"), lax.axis_index("freq")
    freq, strip_index = lax.rem(depth, freqs), lax.div(depth, freqs)
    base = strip_index * strip
    rounds = mine.shape[0]
    spots = kernels * TILE
    span = TAPS * WIN
    rows = [column(stencil[i, pl.ds(freq, 1), :]) for i in range(5)]
    real, imag = lane_taps(rows, column(step[pl.ds(freq, 1), :]), column(shift[pl.ds(freq, 1), :]))
    chunks = wide.shape[0]
    for which, taps in enumerate((real, real + imag, imag - real)):
        taps_high = taps.astype(BF).astype(F32)
        taps_low = taps - taps_high
        rest = jnp.zeros((kernels, chunks * LANES - taps.shape[1]), F32)
        long_high = jnp.concatenate([taps_high, rest], axis=1)
        long_low = jnp.concatenate([taps_low, rest], axis=1)
        line = long_high + pltpu.roll(long_low, span, 1) + pltpu.roll(long_high, 2 * span, 1)
        for row in range(TILE):
            moved = pltpu.roll(line, row, 1) if row else line
            for chunk in range(chunks):
                wide[chunk, pl.ds(row, kernels, stride=TILE), :] = moved[:, chunk * LANES : (chunk + 1) * LANES]
        for chunk in range(chunks):
            weights[which, :, chunk * LANES : (chunk + 1) * LANES] = wide[chunk].astype(BF)
    bins_pad[...] = jnp.full(bins_pad.shape, kernels, jnp.int32)
    for piece, other in ((mine, core), (theirs, 1 - core)):
        for number in range(rounds):
            turn = 1 + number + other * rounds
            bins_pad[lax.rem(depth - turn + 2 * levels, levels), halo : halo + grid, :] = piece[number]
    bins_pad[depth, halo : halo + grid, :] = own[0]
    grid_pad[...] = jnp.zeros(grid_pad.shape, F32)
    for field in range(2):
        for part in range(2):
            grid_pad[2 * field + part, halo : halo + grid, :] = surface[freq, field, :, part * LANES : (part + 1) * LANES]
    lane = lax.broadcasted_iota(jnp.int32, (TILE, LANES), 1)

    def spread(high, low, row, planes):
        parts = []
        for field in range(2):
            re, im = planes[2 * field], planes[2 * field + 1]
            for which, value in enumerate((re + im, im, re)):
                for ref, piece in zip((high, low), split(value)):
                    parts.append((ref, which, field, piece))
        for tap in range(TAPS):
            reach = tap - HALF
            for ref, which, field, piece in parts:
                if reach:
                    piece = pltpu.roll(piece, (-reach) % LANES, 1)
                    inside = lane < LANES - reach if reach > 0 else lane >= -reach
                    piece = jnp.where(inside, piece, jnp.zeros_like(piece))
                ref[which, tap, pl.ds(row, TILE), field * LANES : (field + 1) * LANES] = piece

    def advance(high, low, level, row):
        cell_bins = bins_pad[level, pl.ds(base + HALF * (level + 1) + row, TILE), :]
        sums = []
        for which in range(3):
            rhs = high[which, :, pl.ds(row, WIN), :].reshape(span, 2 * LANES)
            rhs_low = low[which, :, pl.ds(row, WIN), :].reshape(span, 2 * LANES)
            out = jnp.dot(weights[which, :, : 3 * span], jnp.concatenate([rhs, rhs, rhs_low], axis=0), preferred_element_type=F32)
            for field in range(2):
                chosen = jnp.zeros((TILE, LANES), F32)
                for k in range(kernels):
                    chosen = jnp.where(cell_bins == k, out[k * TILE : (k + 1) * TILE, field * LANES : (field + 1) * LANES], chosen)
                sums.append(chosen)
        planes = []
        for field in range(2):
            planes.append(sums[field] - sums[2 + field])
            planes.append(sums[field] + sums[4 + field])
        for plane in range(4):
            state[level % 2, plane, pl.ds(row, TILE), :] = planes[plane]
        return tuple(planes)

    def correlate(level):
        start = halo - HALF * (level + 1)
        planes = [state[level % 2, plane, pl.ds(start, strip), :] for plane in range(4)]
        lanes = lax.broadcasted_iota(jnp.int32, (strip, LANES), 1)
        z, y = level // freqs, level % freqs
        half = image.shape[2]
        place = (lax.rem(z % 2 + core, 2), lax.rem(y + freq, 2), lax.rem(z // 2 + strip_index * (half - 1), half))
        for number in range(lag_count):
            offset = lags[number]
            away = lax.rem(LANES - offset, LANES)
            s_re, s_im = pltpu.roll(planes[0], offset, 1), pltpu.roll(planes[1], offset, 1)
            r_re, r_im = pltpu.roll(planes[2], away, 1), pltpu.roll(planes[3], away, 1)
            inside = (lanes >= offset) & (lanes < LANES - offset)
            image[place[0], place[1], place[2], number] = jnp.where(inside, s_re * r_re + s_im * r_im, 0.0)

    def fill(index, carry):
        row = pl.multiple_of(index * TILE, TILE)
        spread(high0, low0, row, [grid_pad[plane, pl.ds(base + row, TILE), :] for plane in range(4)])
        return carry

    counts = tile_counts(levels, strip)
    lax.fori_loop(0, counts[0] + 1, fill, 0)
    slots = ((high0, low0), (high1, low1))
    planes = None
    for level in range(levels):
        here, there = slots[level % 2], slots[1 - level % 2]
        if planes is None:
            planes = advance(*here, level, 0)
        else:
            last = (counts[level - 1] - 1) * TILE
            if last < WIN:
                spread(*here, last, planes)
                first = advance(*here, level, 0)
            else:
                first = advance(*here, level, 0)
                spread(*here, last, planes)
            correlate(level - 1)
            planes = first

        def tile(number, carried, here=here, there=there, level=level):
            row = number * TILE
            fresh = advance(*here, level, row)
            if level < levels - 1:
                spread(*there, row - TILE, carried)
            return fresh

        for number in range(1, counts[level]):
            planes = tile(number, planes)
    correlate(levels - 1)


def run_levels(lags, surface, own, mine, theirs, stencil, step, shift, strip, levels):
    freqs, _, grid, _ = surface.shape
    kernels = step.shape[1]
    halo = HALF * levels
    rows = (tile_counts(levels, strip)[0] + 1) * TILE
    padded = max((grid - strip + rows + 7) // 8 * 8, halo + grid)
    dims = (levels, kernels, freqs, strip, grid, lags.shape[0])
    half = levels // freqs // 2
    span = -(-3 * TAPS * WIN // LANES)
    vm = pl.BlockSpec(memory_space=pltpu.VMEM)
    sm = pl.BlockSpec(memory_space=pltpu.SMEM)
    operand = pltpu.VMEM((3, TAPS, rows, 2 * LANES), BF)
    return pl.pallas_call(
        functools.partial(levels_kernel, dims),
        out_shape=jax.ShapeDtypeStruct((2, freqs, half, lags.shape[0], strip, grid), F32),
        in_specs=[sm] + [vm] * 7,
        out_specs=vm,
        scratch_shapes=[
            pltpu.VMEM((3, kernels * TILE, span * LANES), BF),
            pltpu.VMEM((span, kernels * TILE, LANES), F32),
            pltpu.VMEM((4, padded, LANES), F32),
            pltpu.VMEM((levels, padded, LANES), jnp.int32),
            operand, operand, operand, operand,
            pltpu.VMEM((2, 4, rows, LANES), F32),
        ],
        compiler_params=pltpu.CompilerParams(vmem_limit_bytes=56 * 1024 * 1024),
    )(lags, surface, own, mine, theirs, jnp.transpose(stencil, (2, 0, 1)), step, shift)


column_tile = 16


def from_behind(value, axis, steps):
    count = lax.axis_size(axis)
    initial, last = (max(0, -steps), min(count, count - steps))
    return lax.ppermute(value, axis, [(source, source + steps) for source in range(initial, last)])


def kernel_taps(stencil, phase_step, phase_shift):
    center = stencil[..., 0]
    along_x = stencil[..., 1]
    along_y = stencil[..., 2]
    diag_main = stencil[..., 3]
    diag_anti = stencil[..., 4]
    row_above = jnp.stack([diag_main, along_y, diag_anti], -1)
    row_middle = jnp.stack([along_x, center, along_x], -1)
    row_below = jnp.stack([diag_anti, along_y, diag_main], -1)
    stencil_grid = jnp.stack([row_above, row_middle, row_below], -2)
    weight_sum = center + 2.0 * (along_x + along_y + diag_main + diag_anti)
    stencil_grid = stencil_grid * (phase_step / weight_sum)[..., None, None]
    lead = stencil.shape[:-1]
    tap_rows = lax.broadcasted_iota(jnp.int32, (TAPS, TAPS), 0)
    tap_cols = lax.broadcasted_iota(jnp.int32, (TAPS, TAPS), 1)
    unit_tap = ((tap_rows == HALF) & (tap_cols == HALF)).astype(jnp.float32)
    power = jnp.broadcast_to(unit_tap, lead + (TAPS, TAPS))
    real_sum = power
    imag_sum = jnp.zeros(lead + (TAPS, TAPS), jnp.float32)
    pad_spec = [(0, 0)] * len(lead) + [(1, 1), (1, 1)]
    for order in range(1, HALF + 1):
        padded = jnp.pad(power, pad_spec)
        grown = jnp.zeros(lead + (TAPS, TAPS), jnp.float32)
        for row_off in range(3):
            for col_off in range(3):
                piece = padded[
                    ..., 2 - row_off : 2 - row_off + TAPS, 2 - col_off : 2 - col_off + TAPS
                ]
                grown = grown + stencil_grid[..., row_off, col_off, None, None] * piece
        power = grown
        weighted = power * (1.0 / math.factorial(order))
        if order % 4 == 1:
            imag_sum = imag_sum + weighted
        elif order % 4 == 2:
            real_sum = real_sum - weighted
        elif order % 4 == 3:
            imag_sum = imag_sum - weighted
        else:
            real_sum = real_sum + weighted
    cosine = jnp.cos(phase_shift)[..., None, None]
    sine = jnp.sin(phase_shift)[..., None, None]
    return (cosine * real_sum - sine * imag_sum, sine * real_sum + cosine * imag_sum)


def advance_level(fields, weights, selector):
    field_count = fields.shape[0]
    grid_width = fields.shape[1]
    tiles = grid_width // column_tile
    parts = fields.reshape(field_count, grid_width, 2, grid_width)
    padded = jnp.pad(parts, ((0, 0), (HALF, HALF), (0, 0), (HALF, column_tile - HALF)))
    main = padded[..., :grid_width].reshape(
        field_count, grid_width + 2 * HALF, 2, tiles, column_tile
    )
    after = padded[..., column_tile : grid_width + column_tile].reshape(
        field_count, grid_width + 2 * HALF, 2, tiles, column_tile
    )
    windows = jnp.concatenate([main, after[..., : 2 * HALF]], -1)
    windows = jnp.transpose(windows, (0, 1, 3, 2, 4))
    patches = jnp.stack(
        [windows[:, row_tap : row_tap + grid_width] for row_tap in range(TAPS)], axis=3
    )
    patches = patches.reshape(field_count * grid_width * tiles, TAPS * 2 * (column_tile + 2 * HALF))
    result = jnp.dot(
        patches, weights, precision=lax.Precision.HIGHEST, preferred_element_type=jnp.float32
    )
    result = result.reshape(field_count, grid_width, tiles, KERNELS, 2, column_tile)
    chosen = jnp.sum(result * selector[None], axis=3)
    return jnp.transpose(chosen, (0, 1, 3, 2, 4)).reshape(field_count, grid_width, 2 * grid_width)


def image_terms(source, receiver, lags):
    grid_width = source.shape[0]
    source_parts = jnp.pad(
        source.reshape(grid_width, 2, grid_width), ((0, 0), (0, 0), (HMAX, HMAX))
    )
    receiver_parts = jnp.pad(
        receiver.reshape(grid_width, 2, grid_width), ((0, 0), (0, 0), (HMAX, HMAX))
    )
    lag_terms = []
    for lag_index in range(LAGS):
        offset = lags[lag_index]
        shifted_source = lax.dynamic_slice_in_dim(source_parts, HMAX - offset, grid_width, 2)
        shifted_receiver = lax.dynamic_slice_in_dim(receiver_parts, HMAX + offset, grid_width, 2)
        lag_terms.append(jnp.sum(shifted_source * shifted_receiver, axis=1))
    return jnp.stack(lag_terms)


def pipeline_body(surface, bins, stencil, phase_step, phase_shift, lags):
    shot_count = surface.shape[0]
    freq_count = surface.shape[1]
    grid_width = surface.shape[3]
    slab_steps = bins.shape[0]
    tiles = grid_width // column_tile
    window_width = column_tile + 2 * HALF
    depth_count = lax.axis_size("depth")
    depth_index = lax.axis_index("depth")
    kern_real, kern_imag = kernel_taps(stencil, phase_step, phase_shift)
    mixing = jnp.stack(
        [jnp.stack([kern_real, kern_imag], 1), jnp.stack([-kern_imag, kern_real], 1)], 1
    )
    window_ids = lax.broadcasted_iota(jnp.int32, (window_width, column_tile, TAPS), 0)
    out_ids = lax.broadcasted_iota(jnp.int32, (window_width, column_tile, TAPS), 1)
    tap_ids = lax.broadcasted_iota(jnp.int32, (window_width, column_tile, TAPS), 2)
    shift_table = (window_ids == out_ids + tap_ids).astype(jnp.float32)
    all_weights = jnp.einsum(
        "fpqkab,cwb->fapckqw", mixing, shift_table, precision=lax.Precision.HIGHEST
    )
    all_weights = all_weights.reshape(
        freq_count, TAPS * 2 * window_width, KERNELS * 2 * column_tile
    )
    kernel_ids = lax.broadcasted_iota(jnp.int32, (1, 1, 1, KERNELS, 1, 1), 3)
    selectors = (
        bins.reshape(slab_steps, grid_width, tiles, 1, 1, column_tile) == kernel_ids
    ).astype(jnp.float32)
    image_part = jnp.zeros((slab_steps, LAGS, grid_width, grid_width), jnp.float32)
    front_count = shot_count * freq_count

    def advance_turn(step_index, carry):
        sent, image_now = carry
        received = from_behind(sent, "depth", 1)
        front_index = step_index - depth_index
        active = (front_index >= 0) & (front_index < front_count)
        clipped = jnp.clip(front_index, 0, front_count - 1)
        shot_index = clipped // freq_count
        freq_index = clipped % freq_count
        shot_fields = lax.dynamic_index_in_dim(surface, shot_index, 0, keepdims=False)
        surface_front = lax.dynamic_index_in_dim(shot_fields, freq_index, 0, keepdims=False)
        incoming = jnp.where(depth_index == 0, surface_front, received)
        weights_front = lax.dynamic_index_in_dim(all_weights, freq_index, 0, keepdims=False)

        def compute_front(state):
            fields, image_held = state
            fields = advance_level(fields, weights_front, selectors[0])
            level_terms = [image_terms(fields[0], fields[1], lags)]
            return (fields, image_held + jnp.stack(level_terms))

        def keep_state(state):
            return state

        return lax.cond(active, compute_front, keep_state, (incoming, image_now))

    start = (jnp.zeros((2, grid_width, 2 * grid_width), jnp.float32), image_part)
    final_sent, image_part = lax.fori_loop(0, depth_count + front_count - 1, advance_turn, start)
    image_part = image_part.reshape(slab_steps, LAGS, grid_width * grid_width)
    return lax.psum_scatter(image_part, "freq", scatter_dimension=2, tiled=True)


def gather_bins(bins):
    count, cores = lax.axis_size("depth"), lax.axis_size("freq")
    rounds = -(-(count - 1) // cores)
    received = []
    for number in range(rounds):
        pairs = []
        for own in range(cores):
            turn = 1 + number + own * rounds
            if turn < count:
                pairs += [(place * cores + own, (place + turn) % count * cores + own) for place in range(count)]
        received.append(lax.ppermute(bins[0], ("depth", "freq"), pairs))
    mine = jnp.stack(received)
    return mine, lax.ppermute(mine, "freq", [(0, 1), (1, 0)])


def spread_image(image, freqs):
    count, cores = lax.axis_size("depth"), lax.axis_size("freq")
    strips = count // freqs
    half = strips // cores
    lags, strip, grid = image.shape[3:]
    block = image[0] + lax.ppermute(image[1], "freq", [(0, 1), (1, 0)])
    block = block[0] + lax.ppermute(block[1], "depth", [(d, d ^ 1) for d in range(count)])
    parts = []
    for number in range(half):
        pairs = []
        for z in range(strips):
            for y in range(freqs):
                for c in range(cores):
                    target = c + cores * ((z % half + number) % half)
                    pairs.append(((z * freqs + y) * cores + c, (target * freqs + y) * cores + z // half))
        parts.append(lax.ppermute(block[number], ("depth", "freq"), pairs))
    stacked = jnp.stack(parts)
    row = lax.axis_index("depth") // freqs // cores
    ordered = jnp.stack([lax.dynamic_index_in_dim(stacked, (row - r) % half, 0, keepdims=False) for r in range(half)], 1)
    return ordered.reshape(1, lags, half * strip * grid)


def strip_body(surface, bins, stencil, phase_step, phase_shift, lags):
    freqs, grid = surface.shape[1], surface.shape[3]
    count = lax.axis_size("depth")
    mine, theirs = gather_bins(bins)
    strip = grid * freqs // count
    image = run_levels(lags, surface[0], bins, mine, theirs, stencil, phase_step, phase_shift, strip, count)
    return spread_image(image, freqs)


def body(surface, bins, stencil, phase_step, phase_shift, lags):
    count, cores = lax.axis_size("depth"), lax.axis_size("freq")
    freqs, grid = surface.shape[1], surface.shape[3]
    strips = count // freqs
    fits = (
        surface.shape[0] == 1
        and bins.shape[0] == 1
        and grid == LANES
        and cores == 2
        and freqs == 2
        and count % freqs == 0
        and strips % cores == 0
        and grid % strips == 0
        and grid // strips % 8 == 0
        and HALF * count <= grid // 2
        and tile_counts(count, grid // strips)[1] < tile_counts(count, grid // strips)[0]
    )
    way = strip_body if fits else pipeline_body
    return way(surface, bins, stencil, phase_step, phase_shift, lags)


def solution(mesh):
    return jax.shard_map(
        body,
        mesh=mesh,
        in_specs=(
            P("shots", "freq", None, None, None),
            P("depth", None, None),
            P("freq", None, None),
            P("freq", None),
            P("freq", None),
            P(),
        ),
        out_specs=P("depth", "shots", "freq"),
        check_vma=False,
    )
```

```python
import functools
import math

import jax
import jax.numpy as jnp
from jax import lax
from jax.experimental import pallas as pl
from jax.experimental.pallas import tpu as pltpu
from jax.sharding import PartitionSpec as P

KERNELS = 8
LAGS = 4
HMAX = 7
TAPS = 13
HALF = 6
TILE = 16
WIN = 32
LANES = 128
BF = jnp.bfloat16
F32 = jnp.float32


def column(row):
    n = row.shape[1]
    eye = lax.broadcasted_iota(jnp.int32, (n, n), 0) == lax.broadcasted_iota(jnp.int32, (n, n), 1)
    return jnp.sum(jnp.where(eye, jnp.broadcast_to(row, (n, n)), 0.0), axis=1, keepdims=True)


def lane_taps(weight, step, shift):
    kernels = step.shape[0]
    lanes = 512
    total = weight[0] + 2.0 * (weight[1] + weight[2] + weight[3] + weight[4])
    scale = step / total
    weight = [w * scale for w in weight]
    lane = lax.broadcasted_iota(jnp.int32, (kernels, lanes), 1)
    power = (lane == HALF * WIN + HALF).astype(F32)
    real, imag = power, jnp.zeros((kernels, lanes), F32)

    def both(value, distance):
        return pltpu.roll(value, distance, 1) + pltpu.roll(value, lanes - distance, 1)

    for order in range(1, HALF + 1):
        power = (
            weight[0] * power
            + weight[1] * both(power, WIN)
            + weight[2] * both(power, 1)
            + weight[3] * both(power, WIN + 1)
            + weight[4] * both(power, WIN - 1)
        )
        term = power * (1.0 / math.factorial(order))
        if order % 4 == 1:
            imag = imag + term
        elif order % 4 == 2:
            real = real - term
        elif order % 4 == 3:
            imag = imag - term
        else:
            real = real + term
    cosine, sine = jnp.cos(shift), jnp.sin(shift)
    return cosine * real - sine * imag, sine * real + cosine * imag


def split(value):
    high = value.astype(BF)
    return high, (value - high.astype(F32)).astype(BF)


def tile_counts(levels, strip):
    return [-(-(strip + 2 * HALF * (levels - 1 - level)) // TILE) for level in range(levels)]


def spread(high, low, row, planes):
    lane = lax.broadcasted_iota(jnp.int32, (TILE, LANES), 1)
    parts = []
    for field in range(2):
        re, im = planes[2 * field], planes[2 * field + 1]
        for which, value in enumerate((re + im, im, re)):
            for ref, piece in zip((high, low), split(value)):
                parts.append((ref, which, field, piece))
    for tap in range(TAPS):
        reach = tap - HALF
        for ref, which, field, piece in parts:
            if reach:
                piece = pltpu.roll(piece, (-reach) % LANES, 1)
                inside = lane < LANES - reach if reach > 0 else lane >= -reach
                piece = jnp.where(inside, piece, jnp.zeros_like(piece))
            ref[which, tap, pl.ds(row, TILE), field * LANES : (field + 1) * LANES] = piece


def distant(value):
    return pltpu.with_memory_space_constraint(value, pltpu.HBM)


def fetch(pairs, sems):
    copies = [pltpu.make_async_copy(source, target, sems.at[number]) for number, (source, target) in enumerate(pairs)]
    for copy in copies:
        copy.start()
    for copy in copies:
        copy.wait()


def weights_kernel(dims, stencil_far, step_far, shift_far, weights, stencil, step, shift, wide, sems):
    levels, kernels, freqs, strip, grid, lag_count = dims
    freq = lax.rem(lax.axis_index("depth"), freqs)
    span = TAPS * WIN
    fetch(((stencil_far, stencil), (step_far, step), (shift_far, shift)), sems)
    rows = [column(stencil[i, pl.ds(freq, 1), :]) for i in range(5)]
    real, imag = lane_taps(rows, column(step[pl.ds(freq, 1), :]), column(shift[pl.ds(freq, 1), :]))
    chunks = wide.shape[0]
    for which, taps in enumerate((real, real + imag, imag - real)):
        taps_high = taps.astype(BF).astype(F32)
        taps_low = taps - taps_high
        rest = jnp.zeros((kernels, chunks * LANES - taps.shape[1]), F32)
        long_high = jnp.concatenate([taps_high, rest], axis=1)
        long_low = jnp.concatenate([taps_low, rest], axis=1)
        line = long_high + pltpu.roll(long_low, span, 1) + pltpu.roll(long_high, 2 * span, 1)
        for row in range(TILE):
            moved = pltpu.roll(line, row, 1) if row else line
            for chunk in range(chunks):
                wide[chunk, pl.ds(row, kernels, stride=TILE), :] = moved[:, chunk * LANES : (chunk + 1) * LANES]
        for chunk in range(chunks):
            weights[which, :, chunk * LANES : (chunk + 1) * LANES] = wide[chunk].astype(BF)


def operands_kernel(dims, surface, high, low, fields, grid_pad, sems):
    levels, kernels, freqs, strip, grid, lag_count = dims
    halo = HALF * levels
    depth = lax.axis_index("depth")
    freq, strip_index = lax.rem(depth, freqs), lax.div(depth, freqs)
    base = strip_index * strip
    fetch(((surface.at[freq], fields),), sems)
    grid_pad[...] = jnp.zeros(grid_pad.shape, F32)
    for field in range(2):
        for part in range(2):
            grid_pad[2 * field + part, halo : halo + grid, :] = fields[field, :, part * LANES : (part + 1) * LANES]

    def fill(index, carry):
        row = pl.multiple_of(index * TILE, TILE)
        spread(high, low, row, [grid_pad[plane, pl.ds(base + row, TILE), :] for plane in range(4)])
        return carry

    lax.fori_loop(0, tile_counts(levels, strip)[0] + 1, fill, 0)


def levels_kernel(dims, lags_far, own, mine, theirs, weights, high, low, image,
                  lags, bins_pad, high0, low0, high1, low1, state, sems):
    levels, kernels, freqs, strip, grid, lag_count = dims
    halo = HALF * levels
    depth, core = lax.axis_index("depth"), lax.axis_index("freq")
    freq, strip_index = lax.rem(depth, freqs), lax.div(depth, freqs)
    base = strip_index * strip
    rounds = mine.shape[0]
    spots = kernels * TILE
    span = TAPS * WIN
    bins_pad[...] = jnp.full(bins_pad.shape, kernels, jnp.int32)
    for piece, other in ((mine, core), (theirs, 1 - core)):
        for number in range(rounds):
            turn = 1 + number + other * rounds
            bins_pad[lax.rem(depth - turn + 2 * levels, levels), halo : halo + grid, :] = piece[number]
    fetch(((lags_far, lags), (own.at[0], bins_pad.at[depth, pl.ds(halo, grid), :])), sems)
    def advance(high, low, level, row):
        cell_bins = bins_pad[level, pl.ds(base + HALF * (level + 1) + row, TILE), :]
        sums = []
        for which in range(3):
            rhs = high[which, :, pl.ds(row, WIN), :].reshape(span, 2 * LANES)
            rhs_low = low[which, :, pl.ds(row, WIN), :].reshape(span, 2 * LANES)
            out = jnp.dot(weights[which, :, : 3 * span], jnp.concatenate([rhs, rhs, rhs_low], axis=0), preferred_element_type=F32)
            for field in range(2):
                chosen = jnp.zeros((TILE, LANES), F32)
                for k in range(kernels):
                    chosen = jnp.where(cell_bins == k, out[k * TILE : (k + 1) * TILE, field * LANES : (field + 1) * LANES], chosen)
                sums.append(chosen)
        planes = []
        for field in range(2):
            planes.append(sums[field] - sums[2 + field])
            planes.append(sums[field] + sums[4 + field])
        for plane in range(4):
            state[level % 2, plane, pl.ds(row, TILE), :] = planes[plane]
        return tuple(planes)

    def correlate(level):
        start = halo - HALF * (level + 1)
        planes = [state[level % 2, plane, pl.ds(start, strip), :] for plane in range(4)]
        lanes = lax.broadcasted_iota(jnp.int32, (strip, LANES), 1)
        z, y = level // freqs, level % freqs
        half = image.shape[2]
        place = (lax.rem(z % 2 + core, 2), lax.rem(y + freq, 2), lax.rem(z // 2 + strip_index * (half - 1), half))
        for number in range(lag_count):
            offset = lags[number]
            away = lax.rem(LANES - offset, LANES)
            s_re, s_im = pltpu.roll(planes[0], offset, 1), pltpu.roll(planes[1], offset, 1)
            r_re, r_im = pltpu.roll(planes[2], away, 1), pltpu.roll(planes[3], away, 1)
            inside = (lanes >= offset) & (lanes < LANES - offset)
            image[place[0], place[1], place[2], number] = jnp.where(inside, s_re * r_re + s_im * r_im, 0.0)

    counts = tile_counts(levels, strip)
    slots = [(high, low), (high1, low1)] + [(high0, low0), (high1, low1)] * levels
    planes = None
    for level in range(levels):
        here, there = slots[level], slots[level + 1]
        if planes is None:
            planes = advance(*here, level, 0)
        else:
            last = (counts[level - 1] - 1) * TILE
            if last < WIN:
                spread(*here, last, planes)
                first = advance(*here, level, 0)
            else:
                first = advance(*here, level, 0)
                spread(*here, last, planes)
            correlate(level - 1)
            planes = first

        def tile(number, carried, here=here, there=there, level=level):
            row = number * TILE
            fresh = advance(*here, level, row)
            if level < levels - 1:
                spread(*there, row - TILE, carried)
            return fresh

        for number in range(1, counts[level]):
            planes = tile(number, planes)
    correlate(levels - 1)


def run_levels(lags, surface, bins, stencil, step, shift, strip, levels):
    freqs, _, grid, _ = surface.shape
    kernels = step.shape[1]
    halo = HALF * levels
    rows = (tile_counts(levels, strip)[0] + 1) * TILE
    padded = max((grid - strip + rows + 7) // 8 * 8, halo + grid)
    dims = (levels, kernels, freqs, strip, grid, lags.shape[0])
    half = levels // freqs // 2
    span = -(-3 * TAPS * WIN // LANES)
    vm = pl.BlockSpec(memory_space=pltpu.VMEM)
    sm = pl.BlockSpec(memory_space=pltpu.SMEM)
    operand = (3, TAPS, rows, 2 * LANES)
    far = pl.BlockSpec(memory_space=pltpu.HBM)
    weights = pl.pallas_call(
        functools.partial(weights_kernel, dims),
        out_shape=jax.ShapeDtypeStruct((3, kernels * TILE, span * LANES), BF),
        in_specs=[far] * 3,
        out_specs=vm,
        scratch_shapes=[
            pltpu.VMEM((5, freqs, kernels), F32),
            pltpu.VMEM((freqs, kernels), F32),
            pltpu.VMEM((freqs, kernels), F32),
            pltpu.VMEM((span, kernels * TILE, LANES), F32),
            pltpu.SemaphoreType.DMA((3,)),
        ],
        compiler_params=pltpu.CompilerParams(vmem_limit_bytes=8 * 1024 * 1024),
    )(*map(distant, (jnp.transpose(stencil, (2, 0, 1)), step, shift)))
    received, weights = lax.optimization_barrier((fetch_bins(bins), weights))
    mine, theirs = swap_bins(received)
    high, low = pl.pallas_call(
        functools.partial(operands_kernel, dims),
        out_shape=[jax.ShapeDtypeStruct(operand, BF)] * 2,
        in_specs=[far],
        out_specs=[vm] * 2,
        scratch_shapes=[
            pltpu.VMEM((2, grid, 2 * grid), F32),
            pltpu.VMEM((4, padded, LANES), F32),
            pltpu.SemaphoreType.DMA((1,)),
        ],
        compiler_params=pltpu.CompilerParams(vmem_limit_bytes=12 * 1024 * 1024),
    )(distant(surface))
    return pl.pallas_call(
        functools.partial(levels_kernel, dims),
        out_shape=jax.ShapeDtypeStruct((2, freqs, half, lags.shape[0], strip, grid), F32),
        in_specs=[far, far] + [vm] * 5,
        out_specs=vm,
        scratch_shapes=[pltpu.SMEM(lags.shape, jnp.int32), pltpu.VMEM((levels, padded, LANES), jnp.int32)]
        + [pltpu.VMEM(operand, BF)] * 4
        + [pltpu.VMEM((2, 4, rows, LANES), F32), pltpu.SemaphoreType.DMA((2,))],
        compiler_params=pltpu.CompilerParams(vmem_limit_bytes=32 * 1024 * 1024),
    )(distant(lags), distant(bins), mine, theirs, weights, high, low)


column_tile = 16


def from_behind(value, axis, steps):
    count = lax.axis_size(axis)
    initial, last = (max(0, -steps), min(count, count - steps))
    return lax.ppermute(value, axis, [(source, source + steps) for source in range(initial, last)])


def kernel_taps(stencil, phase_step, phase_shift):
    center = stencil[..., 0]
    along_x = stencil[..., 1]
    along_y = stencil[..., 2]
    diag_main = stencil[..., 3]
    diag_anti = stencil[..., 4]
    row_above = jnp.stack([diag_main, along_y, diag_anti], -1)
    row_middle = jnp.stack([along_x, center, along_x], -1)
    row_below = jnp.stack([diag_anti, along_y, diag_main], -1)
    stencil_grid = jnp.stack([row_above, row_middle, row_below], -2)
    weight_sum = center + 2.0 * (along_x + along_y + diag_main + diag_anti)
    stencil_grid = stencil_grid * (phase_step / weight_sum)[..., None, None]
    lead = stencil.shape[:-1]
    tap_rows = lax.broadcasted_iota(jnp.int32, (TAPS, TAPS), 0)
    tap_cols = lax.broadcasted_iota(jnp.int32, (TAPS, TAPS), 1)
    unit_tap = ((tap_rows == HALF) & (tap_cols == HALF)).astype(jnp.float32)
    power = jnp.broadcast_to(unit_tap, lead + (TAPS, TAPS))
    real_sum = power
    imag_sum = jnp.zeros(lead + (TAPS, TAPS), jnp.float32)
    pad_spec = [(0, 0)] * len(lead) + [(1, 1), (1, 1)]
    for order in range(1, HALF + 1):
        padded = jnp.pad(power, pad_spec)
        grown = jnp.zeros(lead + (TAPS, TAPS), jnp.float32)
        for row_off in range(3):
            for col_off in range(3):
                piece = padded[
                    ..., 2 - row_off : 2 - row_off + TAPS, 2 - col_off : 2 - col_off + TAPS
                ]
                grown = grown + stencil_grid[..., row_off, col_off, None, None] * piece
        power = grown
        weighted = power * (1.0 / math.factorial(order))
        if order % 4 == 1:
            imag_sum = imag_sum + weighted
        elif order % 4 == 2:
            real_sum = real_sum - weighted
        elif order % 4 == 3:
            imag_sum = imag_sum - weighted
        else:
            real_sum = real_sum + weighted
    cosine = jnp.cos(phase_shift)[..., None, None]
    sine = jnp.sin(phase_shift)[..., None, None]
    return (cosine * real_sum - sine * imag_sum, sine * real_sum + cosine * imag_sum)


def advance_level(fields, weights, selector):
    field_count = fields.shape[0]
    grid_width = fields.shape[1]
    tiles = grid_width // column_tile
    parts = fields.reshape(field_count, grid_width, 2, grid_width)
    padded = jnp.pad(parts, ((0, 0), (HALF, HALF), (0, 0), (HALF, column_tile - HALF)))
    main = padded[..., :grid_width].reshape(
        field_count, grid_width + 2 * HALF, 2, tiles, column_tile
    )
    after = padded[..., column_tile : grid_width + column_tile].reshape(
        field_count, grid_width + 2 * HALF, 2, tiles, column_tile
    )
    windows = jnp.concatenate([main, after[..., : 2 * HALF]], -1)
    windows = jnp.transpose(windows, (0, 1, 3, 2, 4))
    patches = jnp.stack(
        [windows[:, row_tap : row_tap + grid_width] for row_tap in range(TAPS)], axis=3
    )
    patches = patches.reshape(field_count * grid_width * tiles, TAPS * 2 * (column_tile + 2 * HALF))
    result = jnp.dot(
        patches, weights, precision=lax.Precision.HIGHEST, preferred_element_type=jnp.float32
    )
    result = result.reshape(field_count, grid_width, tiles, KERNELS, 2, column_tile)
    chosen = jnp.sum(result * selector[None], axis=3)
    return jnp.transpose(chosen, (0, 1, 3, 2, 4)).reshape(field_count, grid_width, 2 * grid_width)


def image_terms(source, receiver, lags):
    grid_width = source.shape[0]
    source_parts = jnp.pad(
        source.reshape(grid_width, 2, grid_width), ((0, 0), (0, 0), (HMAX, HMAX))
    )
    receiver_parts = jnp.pad(
        receiver.reshape(grid_width, 2, grid_width), ((0, 0), (0, 0), (HMAX, HMAX))
    )
    lag_terms = []
    for lag_index in range(LAGS):
        offset = lags[lag_index]
        shifted_source = lax.dynamic_slice_in_dim(source_parts, HMAX - offset, grid_width, 2)
        shifted_receiver = lax.dynamic_slice_in_dim(receiver_parts, HMAX + offset, grid_width, 2)
        lag_terms.append(jnp.sum(shifted_source * shifted_receiver, axis=1))
    return jnp.stack(lag_terms)


def pipeline_body(surface, bins, stencil, phase_step, phase_shift, lags):
    shot_count = surface.shape[0]
    freq_count = surface.shape[1]
    grid_width = surface.shape[3]
    slab_steps = bins.shape[0]
    tiles = grid_width // column_tile
    window_width = column_tile + 2 * HALF
    depth_count = lax.axis_size("depth")
    depth_index = lax.axis_index("depth")
    kern_real, kern_imag = kernel_taps(stencil, phase_step, phase_shift)
    mixing = jnp.stack(
        [jnp.stack([kern_real, kern_imag], 1), jnp.stack([-kern_imag, kern_real], 1)], 1
    )
    window_ids = lax.broadcasted_iota(jnp.int32, (window_width, column_tile, TAPS), 0)
    out_ids = lax.broadcasted_iota(jnp.int32, (window_width, column_tile, TAPS), 1)
    tap_ids = lax.broadcasted_iota(jnp.int32, (window_width, column_tile, TAPS), 2)
    shift_table = (window_ids == out_ids + tap_ids).astype(jnp.float32)
    all_weights = jnp.einsum(
        "fpqkab,cwb->fapckqw", mixing, shift_table, precision=lax.Precision.HIGHEST
    )
    all_weights = all_weights.reshape(
        freq_count, TAPS * 2 * window_width, KERNELS * 2 * column_tile
    )
    kernel_ids = lax.broadcasted_iota(jnp.int32, (1, 1, 1, KERNELS, 1, 1), 3)
    selectors = (
        bins.reshape(slab_steps, grid_width, tiles, 1, 1, column_tile) == kernel_ids
    ).astype(jnp.float32)
    image_part = jnp.zeros((slab_steps, LAGS, grid_width, grid_width), jnp.float32)
    front_count = shot_count * freq_count

    def advance_turn(step_index, carry):
        sent, image_now = carry
        received = from_behind(sent, "depth", 1)
        front_index = step_index - depth_index
        active = (front_index >= 0) & (front_index < front_count)
        clipped = jnp.clip(front_index, 0, front_count - 1)
        shot_index = clipped // freq_count
        freq_index = clipped % freq_count
        shot_fields = lax.dynamic_index_in_dim(surface, shot_index, 0, keepdims=False)
        surface_front = lax.dynamic_index_in_dim(shot_fields, freq_index, 0, keepdims=False)
        incoming = jnp.where(depth_index == 0, surface_front, received)
        weights_front = lax.dynamic_index_in_dim(all_weights, freq_index, 0, keepdims=False)

        def compute_front(state):
            fields, image_held = state
            fields = advance_level(fields, weights_front, selectors[0])
            level_terms = [image_terms(fields[0], fields[1], lags)]
            return (fields, image_held + jnp.stack(level_terms))

        def keep_state(state):
            return state

        return lax.cond(active, compute_front, keep_state, (incoming, image_now))

    start = (jnp.zeros((2, grid_width, 2 * grid_width), jnp.float32), image_part)
    final_sent, image_part = lax.fori_loop(0, depth_count + front_count - 1, advance_turn, start)
    image_part = image_part.reshape(slab_steps, LAGS, grid_width * grid_width)
    return lax.psum_scatter(image_part, "freq", scatter_dimension=2, tiled=True)


def fetch_bins(bins):
    count, cores = lax.axis_size("depth"), lax.axis_size("freq")
    rounds = -(-(count - 1) // cores)
    received = []
    for number in range(rounds):
        pairs = []
        for own in range(cores):
            turn = 1 + number + own * rounds
            if turn < count:
                pairs += [(place * cores + own, (place + turn) % count * cores + own) for place in range(count)]
        received.append(lax.ppermute(bins[0], ("depth", "freq"), pairs))
    return received


def swap_bins(received):
    mine = jnp.stack(received)
    return mine, lax.ppermute(mine, "freq", [(0, 1), (1, 0)])


def spread_image(image, freqs):
    count, cores = lax.axis_size("depth"), lax.axis_size("freq")
    strips = count // freqs
    half = strips // cores
    lags, strip, grid = image.shape[3:]
    block = image[0] + lax.ppermute(image[1], "freq", [(0, 1), (1, 0)])
    parts = []
    for number in range(half):
        total = None
        for turn in range(freqs):
            pairs = []
            for z in range(strips):
                for y in range(freqs):
                    for c in range(cores):
                        target = c + cores * ((z % half + number) % half)
                        pairs.append(((z * freqs + y) * cores + c, (target * freqs + (y ^ turn)) * cores + z // half))
            part = lax.ppermute(block[turn, number], ("depth", "freq"), pairs)
            total = part if total is None else total + part
        parts.append(total)
    stacked = jnp.stack(parts)
    row = lax.axis_index("depth") // freqs // cores
    ordered = jnp.stack([lax.dynamic_index_in_dim(stacked, (row - r) % half, 0, keepdims=False) for r in range(half)], 1)
    return ordered.reshape(1, lags, half * strip * grid)


def strip_body(surface, bins, stencil, phase_step, phase_shift, lags):
    freqs, grid = surface.shape[1], surface.shape[3]
    count = lax.axis_size("depth")
    strip = grid * freqs // count
    image = run_levels(lags, surface[0], bins, stencil, phase_step, phase_shift, strip, count)
    return spread_image(image, freqs)


def body(surface, bins, stencil, phase_step, phase_shift, lags):
    count, cores = lax.axis_size("depth"), lax.axis_size("freq")
    freqs, grid = surface.shape[1], surface.shape[3]
    strips = count // freqs
    fits = (
        surface.shape[0] == 1
        and bins.shape[0] == 1
        and grid == LANES
        and cores == 2
        and freqs == 2
        and count % freqs == 0
        and strips % cores == 0
        and grid % strips == 0
        and grid // strips % 8 == 0
        and HALF * count <= grid // 2
        and tile_counts(count, grid // strips)[1] < tile_counts(count, grid // strips)[0]
    )
    way = strip_body if fits else pipeline_body
    return way(surface, bins, stencil, phase_step, phase_shift, lags)


def solution(mesh):
    return jax.shard_map(
        body,
        mesh=mesh,
        in_specs=(
            P("shots", "freq", None, None, None),
            P("depth", None, None),
            P("freq", None, None),
            P("freq", None),
            P("freq", None),
            P(),
        ),
        out_specs=P("depth", "shots", "freq"),
        check_vma=False,
    )
```

```python
import functools
import math

import jax
import jax.numpy as jnp
from jax import lax
from jax.experimental import pallas as pl
from jax.experimental.pallas import tpu as pltpu
from jax.sharding import PartitionSpec as P

KERNELS = 8
LAGS = 4
HMAX = 7
TAPS = 13
HALF = 6
TILE = 16
STRIPS = 2
EDGE = 8
WIN = 32
LANES = 128
BF = jnp.bfloat16
F32 = jnp.float32


def column(row):
    n = row.shape[1]
    eye = lax.broadcasted_iota(jnp.int32, (n, n), 0) == lax.broadcasted_iota(jnp.int32, (n, n), 1)
    return jnp.sum(jnp.where(eye, jnp.broadcast_to(row, (n, n)), 0.0), axis=1, keepdims=True)


def lane_taps(weight, step, shift):
    kernels = step.shape[0]
    lanes = 512
    total = weight[0] + 2.0 * (weight[1] + weight[2] + weight[3] + weight[4])
    scale = step / total
    weight = [w * scale for w in weight]
    lane = lax.broadcasted_iota(jnp.int32, (kernels, lanes), 1)
    power = (lane == HALF * WIN + HALF).astype(F32)
    real, imag = power, jnp.zeros((kernels, lanes), F32)

    def both(value, distance):
        return pltpu.roll(value, distance, 1) + pltpu.roll(value, lanes - distance, 1)

    for order in range(1, HALF + 1):
        power = (
            weight[0] * power
            + weight[1] * both(power, WIN)
            + weight[2] * both(power, 1)
            + weight[3] * both(power, WIN + 1)
            + weight[4] * both(power, WIN - 1)
        )
        term = power * (1.0 / math.factorial(order))
        if order % 4 == 1:
            imag = imag + term
        elif order % 4 == 2:
            real = real - term
        elif order % 4 == 3:
            imag = imag - term
        else:
            real = real + term
    cosine, sine = jnp.cos(shift), jnp.sin(shift)
    return cosine * real - sine * imag, sine * real + cosine * imag


def split(value):
    high = value.astype(BF)
    return high, (value - high.astype(F32)).astype(BF)


def tile_counts(levels, grid):
    reaches = [grid // STRIPS + HALF * (levels - 1 - level) for level in range(levels)]
    return [min(-(-reach // TILE), grid // TILE) for reach in reaches]


def spread(high, low, row, planes):
    lane = lax.broadcasted_iota(jnp.int32, (TILE, LANES), 1)
    parts = []
    for field in range(2):
        re, im = planes[2 * field], planes[2 * field + 1]
        for which, value in enumerate((re + im, im, re)):
            for ref, piece in zip((high, low), split(value)):
                parts.append((ref, which, field, piece))
    for tap in range(TAPS):
        reach = tap - HALF
        for ref, which, field, piece in parts:
            if reach:
                piece = pltpu.roll(piece, (-reach) % LANES, 1)
                inside = lane < LANES - reach if reach > 0 else lane >= -reach
                piece = jnp.where(inside, piece, jnp.zeros_like(piece))
            ref[which, tap, pl.ds(row, TILE), field * LANES : (field + 1) * LANES] = piece


def distant(value):
    return pltpu.with_memory_space_constraint(value, pltpu.HBM)


def fetch(pairs, sems):
    copies = [pltpu.make_async_copy(source, target, sems.at[number]) for number, (source, target) in enumerate(pairs)]
    for copy in copies:
        copy.start()
    for copy in copies:
        copy.wait()


def weights_kernel(dims, stencil_far, step_far, shift_far, weights, stencil, step, shift, wide, sems):
    levels, kernels, freqs, grid, lag_count = dims
    freq = lax.rem(lax.axis_index("depth"), freqs)
    span = TAPS * WIN
    fetch(((stencil_far, stencil), (step_far, step), (shift_far, shift)), sems)
    rows = [column(stencil[i, pl.ds(freq, 1), :]) for i in range(5)]
    real, imag = lane_taps(rows, column(step[pl.ds(freq, 1), :]), column(shift[pl.ds(freq, 1), :]))
    chunks = wide.shape[0]
    for which, taps in enumerate((real, real + imag, imag - real)):
        taps_high = taps.astype(BF).astype(F32)
        taps_low = taps - taps_high
        rest = jnp.zeros((kernels, chunks * LANES - taps.shape[1]), F32)
        long_high = jnp.concatenate([taps_high, rest], axis=1)
        long_low = jnp.concatenate([taps_low, rest], axis=1)
        line = long_high + pltpu.roll(long_low, span, 1) + pltpu.roll(long_high, 2 * span, 1)
        for row in range(TILE):
            moved = pltpu.roll(line, row + EDGE - HALF, 1)
            for chunk in range(chunks):
                wide[chunk, pl.ds(row, kernels, stride=TILE), :] = moved[:, chunk * LANES : (chunk + 1) * LANES]
        for chunk in range(chunks):
            weights[which, :, chunk * LANES : (chunk + 1) * LANES] = wide[chunk].astype(BF)


def operands_kernel(dims, surface, high, low, fields, padded, sems):
    levels, kernels, freqs, grid, lag_count = dims
    freq = lax.rem(lax.axis_index("depth"), freqs)
    fetch(((surface.at[freq], fields),), sems)
    for field in range(2):
        for part in range(2):
            plane = 2 * field + part
            padded[plane, :EDGE, :] = jnp.zeros((EDGE, LANES), F32)
            padded[plane, EDGE : EDGE + grid, :] = fields[field, :, part * LANES : (part + 1) * LANES]
            padded[plane, EDGE + grid :, :] = jnp.zeros((EDGE, LANES), F32)

    def fill(index, carry):
        row = pl.multiple_of(index * TILE, TILE)
        spread(high, low, row, [padded[plane, pl.ds(row, TILE), :] for plane in range(4)])
        return carry

    lax.fori_loop(0, grid // TILE + 1, fill, 0)


def levels_kernel(dims, lags_far, own, mine, theirs, weights, high, low, image,
                  lags, bins, high0, low0, high1, low1, state, sems):
    levels, kernels, freqs, grid, lag_count = dims
    depth, core = lax.axis_index("depth"), lax.axis_index("freq")
    freq, layer = lax.rem(depth, freqs), lax.div(depth, freqs)
    strip_index, group = lax.rem(layer, STRIPS), lax.div(layer, STRIPS)
    strip = grid // STRIPS
    span = TAPS * WIN
    counts = tile_counts(levels, grid)
    for piece, other in ((mine, core), (theirs, 1 - core)):
        for number in range(mine.shape[0]):
            turn = 1 + number + other * mine.shape[0]
            bins[lax.rem(depth - turn + 2 * levels, levels)] = piece[number]
    fetch(((lags_far, lags), (own.at[0], bins.at[depth])), sems)

    def descend(forward):
        def row_of(tile):
            return (tile if forward else grid // TILE - 1 - tile) * TILE

        def spread_between(there, number, before, after):
            planes = []
            for old, new in zip(before, after):
                halves = [old[EDGE:], new[:EDGE]] if forward else [new[EDGE:], old[:EDGE]]
                planes.append(jnp.concatenate(halves, axis=0))
            spread(*there, (number if forward else grid // TILE - number) * TILE, planes)

        def advance(high, low, level, row):
            cell_bins = bins[level, pl.ds(row, TILE), :]
            sums = []
            for which in range(3):
                rhs = high[which, :, pl.ds(row, WIN), :].reshape(span, 2 * LANES)
                rhs_low = low[which, :, pl.ds(row, WIN), :].reshape(span, 2 * LANES)
                out = jnp.dot(weights[which, :, : 3 * span], jnp.concatenate([rhs, rhs, rhs_low], axis=0), preferred_element_type=F32)
                for field in range(2):
                    chosen = jnp.zeros((TILE, LANES), F32)
                    for k in range(kernels):
                        chosen = jnp.where(cell_bins == k, out[k * TILE : (k + 1) * TILE, field * LANES : (field + 1) * LANES], chosen)
                    sums.append(chosen)
            planes = []
            for field in range(2):
                planes.append(sums[field] - sums[2 + field])
                planes.append(sums[field] + sums[4 + field])
            for plane in range(4):
                state[level % 2, plane, pl.ds(row, TILE), :] = planes[plane]
            return tuple(planes)

        def correlate(level):
            start = 0 if forward else grid - strip
            planes = [state[level % 2, plane, pl.ds(start, strip), :] for plane in range(4)]
            lanes = lax.broadcasted_iota(jnp.int32, (strip, LANES), 1)
            z, y = level // freqs, level % freqs
            place = (z % STRIPS ^ core) * freqs + (y ^ freq)
            place = jnp.where(group == z // STRIPS, place, STRIPS * freqs)
            for number in range(lag_count):
                offset = lags[number]
                away = lax.rem(LANES - offset, LANES)
                s_re, s_im = pltpu.roll(planes[0], offset, 1), pltpu.roll(planes[1], offset, 1)
                r_re, r_im = pltpu.roll(planes[2], away, 1), pltpu.roll(planes[3], away, 1)
                inside = (lanes >= offset) & (lanes < LANES - offset)
                image[place, number] = jnp.where(inside, s_re * r_re + s_im * r_im, 0.0)

        slots = [(high, low), (high1, low1)] + [(high0, low0), (high1, low1)] * levels
        zeros = tuple(jnp.zeros((TILE, LANES), F32) for _ in range(4))
        before = after = zeros
        for level in range(levels):
            here, there = slots[level], slots[level + 1]
            first = advance(*here, level, row_of(0))
            if level:
                spread_between(here, counts[level - 1] - 1, before, after)
                if counts[level] == counts[level - 1]:
                    spread_between(here, counts[level], after, zeros)
                correlate(level - 1)
            before, after = zeros, first
            for number in range(1, counts[level]):
                fresh = advance(*here, level, row_of(number))
                if level < levels - 1:
                    spread_between(there, number - 1, before, after)
                before, after = after, fresh
        correlate(levels - 1)

    for number in range(STRIPS):

        @pl.when(strip_index == number)
        def _(number=number):
            descend(number == 0)


def run_levels(lags, surface, bins, stencil, step, shift, levels):
    freqs, _, grid, _ = surface.shape
    kernels = step.shape[1]
    rows = grid + 2 * EDGE
    dims = (levels, kernels, freqs, grid, lags.shape[0])
    span = -(-3 * TAPS * WIN // LANES)
    vm = pl.BlockSpec(memory_space=pltpu.VMEM)
    sm = pl.BlockSpec(memory_space=pltpu.SMEM)
    operand = (3, TAPS, rows, 2 * LANES)
    far = pl.BlockSpec(memory_space=pltpu.HBM)
    weights = pl.pallas_call(
        functools.partial(weights_kernel, dims),
        out_shape=jax.ShapeDtypeStruct((3, kernels * TILE, span * LANES), BF),
        in_specs=[far] * 3,
        out_specs=vm,
        scratch_shapes=[
            pltpu.VMEM((5, freqs, kernels), F32),
            pltpu.VMEM((freqs, kernels), F32),
            pltpu.VMEM((freqs, kernels), F32),
            pltpu.VMEM((span, kernels * TILE, LANES), F32),
            pltpu.SemaphoreType.DMA((3,)),
        ],
        compiler_params=pltpu.CompilerParams(vmem_limit_bytes=8 * 1024 * 1024),
    )(*map(distant, (jnp.transpose(stencil, (2, 0, 1)), step, shift)))
    received, weights = lax.optimization_barrier((fetch_bins(bins), weights))
    mine, theirs = swap_bins(received)
    high, low = pl.pallas_call(
        functools.partial(operands_kernel, dims),
        out_shape=[jax.ShapeDtypeStruct(operand, BF)] * 2,
        in_specs=[far],
        out_specs=[vm] * 2,
        scratch_shapes=[
            pltpu.VMEM((2, grid, 2 * grid), F32),
            pltpu.VMEM((4, rows, LANES), F32),
            pltpu.SemaphoreType.DMA((1,)),
        ],
        compiler_params=pltpu.CompilerParams(vmem_limit_bytes=12 * 1024 * 1024),
    )(distant(surface))
    return pl.pallas_call(
        functools.partial(levels_kernel, dims),
        out_shape=jax.ShapeDtypeStruct((STRIPS * freqs + 1, lags.shape[0], grid // STRIPS, grid), F32),
        in_specs=[far, far] + [vm] * 5,
        out_specs=vm,
        scratch_shapes=[pltpu.SMEM(lags.shape, jnp.int32), pltpu.VMEM((levels, grid, LANES), jnp.int32)]
        + [pltpu.VMEM(operand, BF)] * 4
        + [pltpu.VMEM((2, 4, grid, LANES), F32), pltpu.SemaphoreType.DMA((2,))],
        compiler_params=pltpu.CompilerParams(vmem_limit_bytes=32 * 1024 * 1024),
    )(distant(lags), distant(bins), mine, theirs, weights, high, low)


column_tile = 16


def from_behind(value, axis, steps):
    count = lax.axis_size(axis)
    initial, last = (max(0, -steps), min(count, count - steps))
    return lax.ppermute(value, axis, [(source, source + steps) for source in range(initial, last)])


def kernel_taps(stencil, phase_step, phase_shift):
    center = stencil[..., 0]
    along_x = stencil[..., 1]
    along_y = stencil[..., 2]
    diag_main = stencil[..., 3]
    diag_anti = stencil[..., 4]
    row_above = jnp.stack([diag_main, along_y, diag_anti], -1)
    row_middle = jnp.stack([along_x, center, along_x], -1)
    row_below = jnp.stack([diag_anti, along_y, diag_main], -1)
    stencil_grid = jnp.stack([row_above, row_middle, row_below], -2)
    weight_sum = center + 2.0 * (along_x + along_y + diag_main + diag_anti)
    stencil_grid = stencil_grid * (phase_step / weight_sum)[..., None, None]
    lead = stencil.shape[:-1]
    tap_rows = lax.broadcasted_iota(jnp.int32, (TAPS, TAPS), 0)
    tap_cols = lax.broadcasted_iota(jnp.int32, (TAPS, TAPS), 1)
    unit_tap = ((tap_rows == HALF) & (tap_cols == HALF)).astype(jnp.float32)
    power = jnp.broadcast_to(unit_tap, lead + (TAPS, TAPS))
    real_sum = power
    imag_sum = jnp.zeros(lead + (TAPS, TAPS), jnp.float32)
    pad_spec = [(0, 0)] * len(lead) + [(1, 1), (1, 1)]
    for order in range(1, HALF + 1):
        padded = jnp.pad(power, pad_spec)
        grown = jnp.zeros(lead + (TAPS, TAPS), jnp.float32)
        for row_off in range(3):
            for col_off in range(3):
                piece = padded[
                    ..., 2 - row_off : 2 - row_off + TAPS, 2 - col_off : 2 - col_off + TAPS
                ]
                grown = grown + stencil_grid[..., row_off, col_off, None, None] * piece
        power = grown
        weighted = power * (1.0 / math.factorial(order))
        if order % 4 == 1:
            imag_sum = imag_sum + weighted
        elif order % 4 == 2:
            real_sum = real_sum - weighted
        elif order % 4 == 3:
            imag_sum = imag_sum - weighted
        else:
            real_sum = real_sum + weighted
    cosine = jnp.cos(phase_shift)[..., None, None]
    sine = jnp.sin(phase_shift)[..., None, None]
    return (cosine * real_sum - sine * imag_sum, sine * real_sum + cosine * imag_sum)


def advance_level(fields, weights, selector):
    field_count = fields.shape[0]
    grid_width = fields.shape[1]
    tiles = grid_width // column_tile
    parts = fields.reshape(field_count, grid_width, 2, grid_width)
    padded = jnp.pad(parts, ((0, 0), (HALF, HALF), (0, 0), (HALF, column_tile - HALF)))
    main = padded[..., :grid_width].reshape(
        field_count, grid_width + 2 * HALF, 2, tiles, column_tile
    )
    after = padded[..., column_tile : grid_width + column_tile].reshape(
        field_count, grid_width + 2 * HALF, 2, tiles, column_tile
    )
    windows = jnp.concatenate([main, after[..., : 2 * HALF]], -1)
    windows = jnp.transpose(windows, (0, 1, 3, 2, 4))
    patches = jnp.stack(
        [windows[:, row_tap : row_tap + grid_width] for row_tap in range(TAPS)], axis=3
    )
    patches = patches.reshape(field_count * grid_width * tiles, TAPS * 2 * (column_tile + 2 * HALF))
    result = jnp.dot(
        patches, weights, precision=lax.Precision.HIGHEST, preferred_element_type=jnp.float32
    )
    result = result.reshape(field_count, grid_width, tiles, KERNELS, 2, column_tile)
    chosen = jnp.sum(result * selector[None], axis=3)
    return jnp.transpose(chosen, (0, 1, 3, 2, 4)).reshape(field_count, grid_width, 2 * grid_width)


def image_terms(source, receiver, lags):
    grid_width = source.shape[0]
    source_parts = jnp.pad(
        source.reshape(grid_width, 2, grid_width), ((0, 0), (0, 0), (HMAX, HMAX))
    )
    receiver_parts = jnp.pad(
        receiver.reshape(grid_width, 2, grid_width), ((0, 0), (0, 0), (HMAX, HMAX))
    )
    lag_terms = []
    for lag_index in range(LAGS):
        offset = lags[lag_index]
        shifted_source = lax.dynamic_slice_in_dim(source_parts, HMAX - offset, grid_width, 2)
        shifted_receiver = lax.dynamic_slice_in_dim(receiver_parts, HMAX + offset, grid_width, 2)
        lag_terms.append(jnp.sum(shifted_source * shifted_receiver, axis=1))
    return jnp.stack(lag_terms)


def pipeline_body(surface, bins, stencil, phase_step, phase_shift, lags):
    shot_count = surface.shape[0]
    freq_count = surface.shape[1]
    grid_width = surface.shape[3]
    slab_steps = bins.shape[0]
    tiles = grid_width // column_tile
    window_width = column_tile + 2 * HALF
    depth_count = lax.axis_size("depth")
    depth_index = lax.axis_index("depth")
    kern_real, kern_imag = kernel_taps(stencil, phase_step, phase_shift)
    mixing = jnp.stack(
        [jnp.stack([kern_real, kern_imag], 1), jnp.stack([-kern_imag, kern_real], 1)], 1
    )
    window_ids = lax.broadcasted_iota(jnp.int32, (window_width, column_tile, TAPS), 0)
    out_ids = lax.broadcasted_iota(jnp.int32, (window_width, column_tile, TAPS), 1)
    tap_ids = lax.broadcasted_iota(jnp.int32, (window_width, column_tile, TAPS), 2)
    shift_table = (window_ids == out_ids + tap_ids).astype(jnp.float32)
    all_weights = jnp.einsum(
        "fpqkab,cwb->fapckqw", mixing, shift_table, precision=lax.Precision.HIGHEST
    )
    all_weights = all_weights.reshape(
        freq_count, TAPS * 2 * window_width, KERNELS * 2 * column_tile
    )
    kernel_ids = lax.broadcasted_iota(jnp.int32, (1, 1, 1, KERNELS, 1, 1), 3)
    selectors = (
        bins.reshape(slab_steps, grid_width, tiles, 1, 1, column_tile) == kernel_ids
    ).astype(jnp.float32)
    image_part = jnp.zeros((slab_steps, LAGS, grid_width, grid_width), jnp.float32)
    front_count = shot_count * freq_count

    def advance_turn(step_index, carry):
        sent, image_now = carry
        received = from_behind(sent, "depth", 1)
        front_index = step_index - depth_index
        active = (front_index >= 0) & (front_index < front_count)
        clipped = jnp.clip(front_index, 0, front_count - 1)
        shot_index = clipped // freq_count
        freq_index = clipped % freq_count
        shot_fields = lax.dynamic_index_in_dim(surface, shot_index, 0, keepdims=False)
        surface_front = lax.dynamic_index_in_dim(shot_fields, freq_index, 0, keepdims=False)
        incoming = jnp.where(depth_index == 0, surface_front, received)
        weights_front = lax.dynamic_index_in_dim(all_weights, freq_index, 0, keepdims=False)

        def compute_front(state):
            fields, image_held = state
            fields = advance_level(fields, weights_front, selectors[0])
            level_terms = [image_terms(fields[0], fields[1], lags)]
            return (fields, image_held + jnp.stack(level_terms))

        def keep_state(state):
            return state

        return lax.cond(active, compute_front, keep_state, (incoming, image_now))

    start = (jnp.zeros((2, grid_width, 2 * grid_width), jnp.float32), image_part)
    final_sent, image_part = lax.fori_loop(0, depth_count + front_count - 1, advance_turn, start)
    image_part = image_part.reshape(slab_steps, LAGS, grid_width * grid_width)
    return lax.psum_scatter(image_part, "freq", scatter_dimension=2, tiled=True)


def fetch_bins(bins):
    count, cores = lax.axis_size("depth"), lax.axis_size("freq")
    rounds = -(-(count - 1) // cores)
    received = []
    for number in range(rounds):
        pairs = []
        for own in range(cores):
            turn = 1 + number + own * rounds
            if turn < count:
                pairs += [(place * cores + own, (place + turn) % count * cores + own) for place in range(count)]
        received.append(lax.ppermute(bins[0], ("depth", "freq"), pairs))
    return received


def swap_bins(received):
    mine = jnp.stack(received)
    return mine, lax.ppermute(mine, "freq", [(0, 1), (1, 0)])


def spread_image(image, freqs):
    count, cores = lax.axis_size("depth"), lax.axis_size("freq")
    lags, strip, grid = image.shape[1:]
    block = image[:freqs] + lax.ppermute(image[freqs : 2 * freqs], "freq", [(0, 1), (1, 0)])
    total = None
    for turn in reversed(range(freqs)):
        pairs = []
        for depth in range(count):
            z, y = depth // freqs, depth % freqs
            for c in range(cores):
                target = (z // STRIPS * STRIPS + c) * freqs + (y ^ turn)
                pairs.append((depth * cores + c, target * cores + z % STRIPS))
        part = lax.ppermute(block[turn], ("depth", "freq"), pairs)
        total = part if total is None else total + part
    return total.reshape(1, lags, strip * grid)


def strip_body(surface, bins, stencil, phase_step, phase_shift, lags):
    image = run_levels(lags, surface[0], bins, stencil, phase_step, phase_shift, lax.axis_size("depth"))
    return spread_image(image, surface.shape[1])


def body(surface, bins, stencil, phase_step, phase_shift, lags):
    count, cores = lax.axis_size("depth"), lax.axis_size("freq")
    freqs, grid = surface.shape[1], surface.shape[3]
    fits = (
        surface.shape[0] == 1
        and bins.shape[0] == 1
        and grid == LANES
        and cores == 2
        and freqs == 2
        and count % (STRIPS * freqs) == 0
        and count & (count - 1) == 0
        and HALF * (count - 1) <= grid // 2
    )
    way = strip_body if fits else pipeline_body
    return way(surface, bins, stencil, phase_step, phase_shift, lags)


def solution(mesh):
    return jax.shard_map(
        body,
        mesh=mesh,
        in_specs=(
            P("shots", "freq", None, None, None),
            P("depth", None, None),
            P("freq", None, None),
            P("freq", None),
            P("freq", None),
            P(),
        ),
        out_specs=P("depth", "shots", "freq"),
        check_vma=False,
    )
```

```python
import functools
import math

import jax
import jax.numpy as jnp
from jax import lax
from jax.experimental import pallas as pl
from jax.experimental.pallas import tpu as pltpu
from jax.sharding import PartitionSpec as P

KERNELS = 8
LAGS = 4
HMAX = 7
TAPS = 13
HALF = 6
TILE = 16
STRIPS = 2
EDGE = 8
WIN = 32
LANES = 128
BF = jnp.bfloat16
F32 = jnp.float32


def column(row):
    n = row.shape[1]
    eye = lax.broadcasted_iota(jnp.int32, (n, n), 0) == lax.broadcasted_iota(jnp.int32, (n, n), 1)
    return jnp.sum(jnp.where(eye, jnp.broadcast_to(row, (n, n)), 0.0), axis=1, keepdims=True)


def lane_taps(weight, step, shift):
    kernels = step.shape[0]
    lanes = 512
    total = weight[0] + 2.0 * (weight[1] + weight[2] + weight[3] + weight[4])
    scale = step / total
    weight = [w * scale for w in weight]
    lane = lax.broadcasted_iota(jnp.int32, (kernels, lanes), 1)
    power = (lane == HALF * WIN + HALF).astype(F32)
    real, imag = power, jnp.zeros((kernels, lanes), F32)

    def both(value, distance):
        return pltpu.roll(value, distance, 1) + pltpu.roll(value, lanes - distance, 1)

    for order in range(1, HALF + 1):
        power = (
            weight[0] * power
            + weight[1] * both(power, WIN)
            + weight[2] * both(power, 1)
            + weight[3] * both(power, WIN + 1)
            + weight[4] * both(power, WIN - 1)
        )
        term = power * (1.0 / math.factorial(order))
        if order % 4 == 1:
            imag = imag + term
        elif order % 4 == 2:
            real = real - term
        elif order % 4 == 3:
            imag = imag - term
        else:
            real = real + term
    cosine, sine = jnp.cos(shift), jnp.sin(shift)
    return cosine * real - sine * imag, sine * real + cosine * imag


def split(value):
    high = value.astype(BF)
    return high, (value - high.astype(F32)).astype(BF)


def tile_counts(levels, grid):
    reaches = [grid // STRIPS + HALF * (levels - 1 - level) for level in range(levels)]
    return [min(-(-reach // TILE), grid // TILE) for reach in reaches]


def spread(high, low, row, planes):
    lane = lax.broadcasted_iota(jnp.int32, (TILE, LANES), 1)
    parts = []
    for field in range(2):
        re, im = planes[2 * field], planes[2 * field + 1]
        for which, value in enumerate((re + im, im, re)):
            for ref, piece in zip((high, low), split(value)):
                parts.append((ref, which, field, piece))
    for tap in range(TAPS):
        reach = tap - HALF
        for ref, which, field, piece in parts:
            if reach:
                piece = pltpu.roll(piece, (-reach) % LANES, 1)
                inside = lane < LANES - reach if reach > 0 else lane >= -reach
                piece = jnp.where(inside, piece, jnp.zeros_like(piece))
            ref[which, tap, pl.ds(row, TILE), field * LANES : (field + 1) * LANES] = piece


def distant(value):
    return pltpu.with_memory_space_constraint(value, pltpu.HBM)


def fetch(pairs, sems):
    copies = [pltpu.make_async_copy(source, target, sems.at[number]) for number, (source, target) in enumerate(pairs)]
    for copy in copies:
        copy.start()
    for copy in copies:
        copy.wait()


def weights_kernel(dims, stencil_far, step_far, shift_far, weights, stencil, step, shift, wide, sems):
    levels, kernels, freqs, grid, lag_count = dims
    freq = lax.rem(lax.axis_index("depth"), freqs)
    span = TAPS * WIN
    fetch(((stencil_far, stencil), (step_far, step), (shift_far, shift)), sems)
    rows = [column(stencil[i, pl.ds(freq, 1), :]) for i in range(5)]
    real, imag = lane_taps(rows, column(step[pl.ds(freq, 1), :]), column(shift[pl.ds(freq, 1), :]))
    chunks = wide.shape[0]
    for which, taps in enumerate((real, real + imag, imag - real)):
        taps_high = taps.astype(BF).astype(F32)
        taps_low = taps - taps_high
        rest = jnp.zeros((kernels, chunks * LANES - taps.shape[1]), F32)
        long_high = jnp.concatenate([taps_high, rest], axis=1)
        long_low = jnp.concatenate([taps_low, rest], axis=1)
        line = long_high + pltpu.roll(long_low, span, 1) + pltpu.roll(long_high, 2 * span, 1)
        for row in range(TILE):
            moved = pltpu.roll(line, row + EDGE - HALF, 1)
            for chunk in range(chunks):
                wide[chunk, pl.ds(row, kernels, stride=TILE), :] = moved[:, chunk * LANES : (chunk + 1) * LANES]
        for chunk in range(chunks):
            weights[which, :, chunk * LANES : (chunk + 1) * LANES] = wide[chunk].astype(BF)


def operands_kernel(dims, surface, high, low, fields, padded, sems):
    levels, kernels, freqs, grid, lag_count = dims
    freq = lax.rem(lax.axis_index("depth"), freqs)
    fetch(((surface.at[freq], fields),), sems)
    for field in range(2):
        for part in range(2):
            plane = 2 * field + part
            padded[plane, :EDGE, :] = jnp.zeros((EDGE, LANES), F32)
            padded[plane, EDGE : EDGE + grid, :] = fields[field, :, part * LANES : (part + 1) * LANES]
            padded[plane, EDGE + grid :, :] = jnp.zeros((EDGE, LANES), F32)

    for row in range(0, grid + 1, TILE):
        spread(high, low, row, [padded[plane, pl.ds(row, TILE), :] for plane in range(4)])


def levels_kernel(dims, lags_far, own, mine, theirs, weights, high, low, image,
                  lags, bins, high0, low0, high1, low1, state, sems):
    levels, kernels, freqs, grid, lag_count = dims
    depth, core = lax.axis_index("depth"), lax.axis_index("freq")
    freq, layer = lax.rem(depth, freqs), lax.div(depth, freqs)
    strip_index, group = lax.rem(layer, STRIPS), lax.div(layer, STRIPS)
    strip = grid // STRIPS
    span = TAPS * WIN
    counts = tile_counts(levels, grid)
    for piece, other in ((mine, core), (theirs, 1 - core)):
        for number in range(mine.shape[0]):
            turn = 1 + number + other * mine.shape[0]
            bins[lax.rem(depth - turn + 2 * levels, levels)] = piece[number]
    fetch(((lags_far, lags), (own.at[0], bins.at[depth])), sems)

    def descend(forward):
        def row_of(tile):
            return (tile if forward else grid // TILE - 1 - tile) * TILE

        def spread_between(there, number, before, after):
            planes = []
            for old, new in zip(before, after):
                halves = [old[EDGE:], new[:EDGE]] if forward else [new[EDGE:], old[:EDGE]]
                planes.append(jnp.concatenate(halves, axis=0))
            spread(*there, (number if forward else grid // TILE - number) * TILE, planes)

        def advance(high, low, level, row):
            cell_bins = bins[level, pl.ds(row, TILE), :]
            sums = []
            for which in range(3):
                rhs = high[which, :, pl.ds(row, WIN), :].reshape(span, 2 * LANES)
                rhs_low = low[which, :, pl.ds(row, WIN), :].reshape(span, 2 * LANES)
                out = jnp.dot(weights[which, :, : 3 * span], jnp.concatenate([rhs, rhs, rhs_low], axis=0), preferred_element_type=F32)
                for field in range(2):
                    chosen = jnp.zeros((TILE, LANES), F32)
                    for k in range(kernels):
                        chosen = jnp.where(cell_bins == k, out[k * TILE : (k + 1) * TILE, field * LANES : (field + 1) * LANES], chosen)
                    sums.append(chosen)
            planes = []
            for field in range(2):
                planes.append(sums[field] - sums[2 + field])
                planes.append(sums[field] + sums[4 + field])
            for plane in range(4):
                state[level % 2, plane, pl.ds(row, TILE), :] = planes[plane]
            return tuple(planes)

        def correlate(level):
            start = 0 if forward else grid - strip
            planes = [state[level % 2, plane, pl.ds(start, strip), :] for plane in range(4)]
            lanes = lax.broadcasted_iota(jnp.int32, (strip, LANES), 1)
            z, y = level // freqs, level % freqs
            place = (z % STRIPS ^ core) * freqs + (y ^ freq)
            place = jnp.where(group == z // STRIPS, place, STRIPS * freqs)
            for number in range(lag_count):
                offset = lags[number]
                away = lax.rem(LANES - offset, LANES)
                s_re, s_im = pltpu.roll(planes[0], offset, 1), pltpu.roll(planes[1], offset, 1)
                r_re, r_im = pltpu.roll(planes[2], away, 1), pltpu.roll(planes[3], away, 1)
                inside = (lanes >= offset) & (lanes < LANES - offset)
                image[place, pl.ds(number, strip, stride=lag_count), :] = jnp.where(inside, s_re * r_re + s_im * r_im, 0.0)

        slots = [(high, low), (high1, low1)] + [(high0, low0), (high1, low1)] * levels
        zeros = tuple(jnp.zeros((TILE, LANES), F32) for _ in range(4))
        before = after = zeros
        for level in range(levels):
            here, there = slots[level], slots[level + 1]
            first = advance(*here, level, row_of(0))
            if level:
                spread_between(here, counts[level - 1] - 1, before, after)
                if counts[level] == counts[level - 1]:
                    spread_between(here, counts[level], after, zeros)
                correlate(level - 1)
            before, after = zeros, first
            for number in range(1, counts[level]):
                fresh = advance(*here, level, row_of(number))
                if level < levels - 1:
                    spread_between(there, number - 1, before, after)
                before, after = after, fresh
        correlate(levels - 1)

    for number in range(STRIPS):

        @pl.when(strip_index == number)
        def _(number=number):
            descend(number == 0)


def run_levels(lags, surface, bins, stencil, step, shift, levels):
    freqs, _, grid, _ = surface.shape
    kernels = step.shape[1]
    rows = grid + 2 * EDGE
    dims = (levels, kernels, freqs, grid, lags.shape[0])
    span = -(-3 * TAPS * WIN // LANES)
    vm = pl.BlockSpec(memory_space=pltpu.VMEM)
    sm = pl.BlockSpec(memory_space=pltpu.SMEM)
    operand = (3, TAPS, rows, 2 * LANES)
    far = pl.BlockSpec(memory_space=pltpu.HBM)
    weights = pl.pallas_call(
        functools.partial(weights_kernel, dims),
        out_shape=jax.ShapeDtypeStruct((3, kernels * TILE, span * LANES), BF),
        in_specs=[far] * 3,
        out_specs=vm,
        scratch_shapes=[
            pltpu.VMEM((5, freqs, kernels), F32),
            pltpu.VMEM((freqs, kernels), F32),
            pltpu.VMEM((freqs, kernels), F32),
            pltpu.VMEM((span, kernels * TILE, LANES), F32),
            pltpu.SemaphoreType.DMA((3,)),
        ],
        compiler_params=pltpu.CompilerParams(vmem_limit_bytes=8 * 1024 * 1024),
    )(*map(distant, (jnp.transpose(stencil, (2, 0, 1)), step, shift)))
    high, low = pl.pallas_call(
        functools.partial(operands_kernel, dims),
        out_shape=[jax.ShapeDtypeStruct(operand, BF)] * 2,
        in_specs=[far],
        out_specs=[vm] * 2,
        scratch_shapes=[
            pltpu.VMEM((2, grid, 2 * grid), F32),
            pltpu.VMEM((4, rows, LANES), F32),
            pltpu.SemaphoreType.DMA((1,)),
        ],
        compiler_params=pltpu.CompilerParams(vmem_limit_bytes=12 * 1024 * 1024),
    )(distant(surface))
    received, weights, high, low = lax.optimization_barrier((fetch_bins(bins), weights, high, low))
    mine, theirs = swap_bins(received)
    return pl.pallas_call(
        functools.partial(levels_kernel, dims),
        out_shape=jax.ShapeDtypeStruct((STRIPS * freqs + 1, grid // STRIPS * lags.shape[0], grid), F32),
        in_specs=[far, far] + [vm] * 5,
        out_specs=vm,
        scratch_shapes=[pltpu.SMEM(lags.shape, jnp.int32), pltpu.VMEM((levels, grid, LANES), jnp.int32)]
        + [pltpu.VMEM(operand, BF)] * 4
        + [pltpu.VMEM((2, 4, grid, LANES), F32), pltpu.SemaphoreType.DMA((2,))],
        compiler_params=pltpu.CompilerParams(vmem_limit_bytes=32 * 1024 * 1024),
    )(distant(lags), distant(bins), mine, theirs, weights, high, low)


column_tile = 16


def from_behind(value, axis, steps):
    count = lax.axis_size(axis)
    initial, last = (max(0, -steps), min(count, count - steps))
    return lax.ppermute(value, axis, [(source, source + steps) for source in range(initial, last)])


def kernel_taps(stencil, phase_step, phase_shift):
    center = stencil[..., 0]
    along_x = stencil[..., 1]
    along_y = stencil[..., 2]
    diag_main = stencil[..., 3]
    diag_anti = stencil[..., 4]
    row_above = jnp.stack([diag_main, along_y, diag_anti], -1)
    row_middle = jnp.stack([along_x, center, along_x], -1)
    row_below = jnp.stack([diag_anti, along_y, diag_main], -1)
    stencil_grid = jnp.stack([row_above, row_middle, row_below], -2)
    weight_sum = center + 2.0 * (along_x + along_y + diag_main + diag_anti)
    stencil_grid = stencil_grid * (phase_step / weight_sum)[..., None, None]
    lead = stencil.shape[:-1]
    tap_rows = lax.broadcasted_iota(jnp.int32, (TAPS, TAPS), 0)
    tap_cols = lax.broadcasted_iota(jnp.int32, (TAPS, TAPS), 1)
    unit_tap = ((tap_rows == HALF) & (tap_cols == HALF)).astype(jnp.float32)
    power = jnp.broadcast_to(unit_tap, lead + (TAPS, TAPS))
    real_sum = power
    imag_sum = jnp.zeros(lead + (TAPS, TAPS), jnp.float32)
    pad_spec = [(0, 0)] * len(lead) + [(1, 1), (1, 1)]
    for order in range(1, HALF + 1):
        padded = jnp.pad(power, pad_spec)
        grown = jnp.zeros(lead + (TAPS, TAPS), jnp.float32)
        for row_off in range(3):
            for col_off in range(3):
                piece = padded[
                    ..., 2 - row_off : 2 - row_off + TAPS, 2 - col_off : 2 - col_off + TAPS
                ]
                grown = grown + stencil_grid[..., row_off, col_off, None, None] * piece
        power = grown
        weighted = power * (1.0 / math.factorial(order))
        if order % 4 == 1:
            imag_sum = imag_sum + weighted
        elif order % 4 == 2:
            real_sum = real_sum - weighted
        elif order % 4 == 3:
            imag_sum = imag_sum - weighted
        else:
            real_sum = real_sum + weighted
    cosine = jnp.cos(phase_shift)[..., None, None]
    sine = jnp.sin(phase_shift)[..., None, None]
    return (cosine * real_sum - sine * imag_sum, sine * real_sum + cosine * imag_sum)


def advance_level(fields, weights, selector):
    field_count = fields.shape[0]
    grid_width = fields.shape[1]
    tiles = grid_width // column_tile
    parts = fields.reshape(field_count, grid_width, 2, grid_width)
    padded = jnp.pad(parts, ((0, 0), (HALF, HALF), (0, 0), (HALF, column_tile - HALF)))
    main = padded[..., :grid_width].reshape(
        field_count, grid_width + 2 * HALF, 2, tiles, column_tile
    )
    after = padded[..., column_tile : grid_width + column_tile].reshape(
        field_count, grid_width + 2 * HALF, 2, tiles, column_tile
    )
    windows = jnp.concatenate([main, after[..., : 2 * HALF]], -1)
    windows = jnp.transpose(windows, (0, 1, 3, 2, 4))
    patches = jnp.stack(
        [windows[:, row_tap : row_tap + grid_width] for row_tap in range(TAPS)], axis=3
    )
    patches = patches.reshape(field_count * grid_width * tiles, TAPS * 2 * (column_tile + 2 * HALF))
    result = jnp.dot(
        patches, weights, precision=lax.Precision.HIGHEST, preferred_element_type=jnp.float32
    )
    result = result.reshape(field_count, grid_width, tiles, KERNELS, 2, column_tile)
    chosen = jnp.sum(result * selector[None], axis=3)
    return jnp.transpose(chosen, (0, 1, 3, 2, 4)).reshape(field_count, grid_width, 2 * grid_width)


def image_terms(source, receiver, lags):
    grid_width = source.shape[0]
    source_parts = jnp.pad(
        source.reshape(grid_width, 2, grid_width), ((0, 0), (0, 0), (HMAX, HMAX))
    )
    receiver_parts = jnp.pad(
        receiver.reshape(grid_width, 2, grid_width), ((0, 0), (0, 0), (HMAX, HMAX))
    )
    lag_terms = []
    for lag_index in range(LAGS):
        offset = lags[lag_index]
        shifted_source = lax.dynamic_slice_in_dim(source_parts, HMAX - offset, grid_width, 2)
        shifted_receiver = lax.dynamic_slice_in_dim(receiver_parts, HMAX + offset, grid_width, 2)
        lag_terms.append(jnp.sum(shifted_source * shifted_receiver, axis=1))
    return jnp.stack(lag_terms)


def pipeline_body(surface, bins, stencil, phase_step, phase_shift, lags):
    shot_count = surface.shape[0]
    freq_count = surface.shape[1]
    grid_width = surface.shape[3]
    slab_steps = bins.shape[0]
    tiles = grid_width // column_tile
    window_width = column_tile + 2 * HALF
    depth_count = lax.axis_size("depth")
    depth_index = lax.axis_index("depth")
    kern_real, kern_imag = kernel_taps(stencil, phase_step, phase_shift)
    mixing = jnp.stack(
        [jnp.stack([kern_real, kern_imag], 1), jnp.stack([-kern_imag, kern_real], 1)], 1
    )
    window_ids = lax.broadcasted_iota(jnp.int32, (window_width, column_tile, TAPS), 0)
    out_ids = lax.broadcasted_iota(jnp.int32, (window_width, column_tile, TAPS), 1)
    tap_ids = lax.broadcasted_iota(jnp.int32, (window_width, column_tile, TAPS), 2)
    shift_table = (window_ids == out_ids + tap_ids).astype(jnp.float32)
    all_weights = jnp.einsum(
        "fpqkab,cwb->fapckqw", mixing, shift_table, precision=lax.Precision.HIGHEST
    )
    all_weights = all_weights.reshape(
        freq_count, TAPS * 2 * window_width, KERNELS * 2 * column_tile
    )
    kernel_ids = lax.broadcasted_iota(jnp.int32, (1, 1, 1, KERNELS, 1, 1), 3)
    selectors = (
        bins.reshape(slab_steps, grid_width, tiles, 1, 1, column_tile) == kernel_ids
    ).astype(jnp.float32)
    image_part = jnp.zeros((slab_steps, LAGS, grid_width, grid_width), jnp.float32)
    front_count = shot_count * freq_count

    def advance_turn(step_index, carry):
        sent, image_now = carry
        received = from_behind(sent, "depth", 1)
        front_index = step_index - depth_index
        active = (front_index >= 0) & (front_index < front_count)
        clipped = jnp.clip(front_index, 0, front_count - 1)
        shot_index = clipped // freq_count
        freq_index = clipped % freq_count
        shot_fields = lax.dynamic_index_in_dim(surface, shot_index, 0, keepdims=False)
        surface_front = lax.dynamic_index_in_dim(shot_fields, freq_index, 0, keepdims=False)
        incoming = jnp.where(depth_index == 0, surface_front, received)
        weights_front = lax.dynamic_index_in_dim(all_weights, freq_index, 0, keepdims=False)

        def compute_front(state):
            fields, image_held = state
            fields = advance_level(fields, weights_front, selectors[0])
            level_terms = [image_terms(fields[0], fields[1], lags)]
            return (fields, image_held + jnp.stack(level_terms))

        def keep_state(state):
            return state

        return lax.cond(active, compute_front, keep_state, (incoming, image_now))

    start = (jnp.zeros((2, grid_width, 2 * grid_width), jnp.float32), image_part)
    final_sent, image_part = lax.fori_loop(0, depth_count + front_count - 1, advance_turn, start)
    image_part = image_part.reshape(slab_steps, LAGS, grid_width * grid_width)
    return lax.psum_scatter(image_part, "freq", scatter_dimension=2, tiled=True)


def fetch_bins(bins):
    count, cores = lax.axis_size("depth"), lax.axis_size("freq")
    rounds = -(-(count - 1) // cores)
    received = []
    for number in range(rounds):
        pairs = []
        for own in range(cores):
            turn = 1 + number + own * rounds
            if turn < count:
                pairs += [(place * cores + own, (place + turn) % count * cores + own) for place in range(count)]
        received.append(lax.ppermute(bins[0], ("depth", "freq"), pairs))
    return received


def swap_bins(received):
    mine = jnp.stack(received)
    return mine, lax.ppermute(mine, "freq", [(0, 1), (1, 0)])


def spread_image(image, freqs, lags):
    count, cores = lax.axis_size("depth"), lax.axis_size("freq")
    grid = image.shape[2]
    block = image[:freqs] + lax.ppermute(image[freqs : 2 * freqs], "freq", [(0, 1), (1, 0)])
    total = None
    for turn in reversed(range(freqs)):
        pairs = []
        for depth in range(count):
            z, y = depth // freqs, depth % freqs
            for c in range(cores):
                target = (z // STRIPS * STRIPS + c) * freqs + (y ^ turn)
                pairs.append((depth * cores + c, target * cores + z % STRIPS))
        part = lax.ppermute(block[turn], ("depth", "freq"), pairs)
        total = part if total is None else total + part
    total = jnp.transpose(total.reshape(-1, lags, grid), (1, 0, 2))
    return total.reshape(1, lags, -1)


def strip_body(surface, bins, stencil, phase_step, phase_shift, lags):
    image = run_levels(lags, surface[0], bins, stencil, phase_step, phase_shift, lax.axis_size("depth"))
    return spread_image(image, surface.shape[1], lags.shape[0])


def body(surface, bins, stencil, phase_step, phase_shift, lags):
    count, cores = lax.axis_size("depth"), lax.axis_size("freq")
    freqs, grid = surface.shape[1], surface.shape[3]
    fits = (
        surface.shape[0] == 1
        and bins.shape[0] == 1
        and grid == LANES
        and cores == 2
        and freqs == 2
        and count % (STRIPS * freqs) == 0
        and count & (count - 1) == 0
        and HALF * (count - 1) <= grid // 2
    )
    way = strip_body if fits else pipeline_body
    return way(surface, bins, stencil, phase_step, phase_shift, lags)


def solution(mesh):
    return jax.shard_map(
        body,
        mesh=mesh,
        in_specs=(
            P("shots", "freq", None, None, None),
            P("depth", None, None),
            P("freq", None, None),
            P("freq", None),
            P("freq", None),
            P(),
        ),
        out_specs=P("depth", "shots", "freq"),
        check_vma=False,
    )
```

```python
import functools
import math

import jax
import jax.numpy as jnp
from jax import lax
from jax.experimental import pallas as pl
from jax.experimental.pallas import tpu as pltpu
from jax.sharding import PartitionSpec as P

KERNELS = 8
LAGS = 4
HMAX = 7
TAPS = 13
HALF = 6
TILE = 16
STRIPS = 2
EDGE = 8
WIN = 32
LANES = 128
BF = jnp.bfloat16
F32 = jnp.float32


def column(row):
    n = row.shape[1]
    eye = lax.broadcasted_iota(jnp.int32, (n, n), 0) == lax.broadcasted_iota(jnp.int32, (n, n), 1)
    return jnp.sum(jnp.where(eye, jnp.broadcast_to(row, (n, n)), 0.0), axis=1, keepdims=True)


def lane_taps(weight, step, shift):
    kernels = step.shape[0]
    lanes = 512
    total = weight[0] + 2.0 * (weight[1] + weight[2] + weight[3] + weight[4])
    scale = step / total
    weight = [w * scale for w in weight]
    lane = lax.broadcasted_iota(jnp.int32, (kernels, lanes), 1)
    power = (lane == HALF * WIN + HALF).astype(F32)
    real, imag = power, jnp.zeros((kernels, lanes), F32)

    def both(value, distance):
        return pltpu.roll(value, distance, 1) + pltpu.roll(value, lanes - distance, 1)

    for order in range(1, HALF + 1):
        power = (
            weight[0] * power
            + weight[1] * both(power, WIN)
            + weight[2] * both(power, 1)
            + weight[3] * both(power, WIN + 1)
            + weight[4] * both(power, WIN - 1)
        )
        term = power * (1.0 / math.factorial(order))
        if order % 4 == 1:
            imag = imag + term
        elif order % 4 == 2:
            real = real - term
        elif order % 4 == 3:
            imag = imag - term
        else:
            real = real + term
    cosine, sine = jnp.cos(shift), jnp.sin(shift)
    return cosine * real - sine * imag, sine * real + cosine * imag


def split(value):
    high = value.astype(BF)
    return high, (value - high.astype(F32)).astype(BF)


def tile_counts(levels, grid):
    reaches = [grid // STRIPS + HALF * (levels - 1 - level) for level in range(levels)]
    return [min(-(-reach // TILE), grid // TILE) for reach in reaches]


def spread(high, low, row, planes):
    lane = lax.broadcasted_iota(jnp.int32, (TILE, LANES), 1)
    parts = []
    for field in range(2):
        re, im = planes[2 * field], planes[2 * field + 1]
        for which, value in enumerate((re + im, im, re)):
            for ref, piece in zip((high, low), split(value)):
                parts.append((ref, which, field, piece))
    for tap in range(TAPS):
        reach = tap - HALF
        for ref, which, field, piece in parts:
            if reach:
                piece = pltpu.roll(piece, (-reach) % LANES, 1)
                inside = lane < LANES - reach if reach > 0 else lane >= -reach
                piece = jnp.where(inside, piece, jnp.zeros_like(piece))
            ref[which, tap, pl.ds(row, TILE), field * LANES : (field + 1) * LANES] = piece


def distant(value):
    return pltpu.with_memory_space_constraint(value, pltpu.HBM)


def fetch(pairs, sems):
    copies = [pltpu.make_async_copy(source, target, sems.at[number]) for number, (source, target) in enumerate(pairs)]
    for copy in copies:
        copy.start()
    for copy in copies:
        copy.wait()


def weights_kernel(dims, stencil_far, step_far, shift_far, weights, stencil, step, shift, wide, sems):
    levels, kernels, freqs, grid, lag_count = dims
    freq = lax.rem(lax.axis_index("depth"), freqs)
    span = TAPS * WIN
    fetch(((stencil_far, stencil), (step_far, step), (shift_far, shift)), sems)
    rows = [column(stencil[i, pl.ds(freq, 1), :]) for i in range(5)]
    real, imag = lane_taps(rows, column(step[pl.ds(freq, 1), :]), column(shift[pl.ds(freq, 1), :]))
    chunks = wide.shape[0]
    for which, taps in enumerate((real, real + imag, imag - real)):
        taps_high = taps.astype(BF).astype(F32)
        taps_low = taps - taps_high
        rest = jnp.zeros((kernels, chunks * LANES - taps.shape[1]), F32)
        long_high = jnp.concatenate([taps_high, rest], axis=1)
        long_low = jnp.concatenate([taps_low, rest], axis=1)
        line = long_high + pltpu.roll(long_low, span, 1) + pltpu.roll(long_high, 2 * span, 1)
        for row in range(TILE):
            moved = pltpu.roll(line, row + EDGE - HALF, 1)
            for chunk in range(chunks):
                wide[chunk, pl.ds(row, kernels, stride=TILE), :] = moved[:, chunk * LANES : (chunk + 1) * LANES]
        for chunk in range(chunks):
            weights[which, :, chunk * LANES : (chunk + 1) * LANES] = wide[chunk].astype(BF)


def operands_kernel(dims, surface, high, low, fields, padded, sems):
    levels, kernels, freqs, grid, lag_count = dims
    freq = lax.rem(lax.axis_index("depth"), freqs)
    fetch(((surface.at[freq], fields),), sems)
    for field in range(2):
        for part in range(2):
            plane = 2 * field + part
            padded[plane, :EDGE, :] = jnp.zeros((EDGE, LANES), F32)
            padded[plane, EDGE : EDGE + grid, :] = fields[field, :, part * LANES : (part + 1) * LANES]
            padded[plane, EDGE + grid :, :] = jnp.zeros((EDGE, LANES), F32)

    for row in range(0, grid + 1, TILE):
        spread(high, low, row, [padded[plane, pl.ds(row, TILE), :] for plane in range(4)])


def levels_kernel(dims, lags_far, own, mine, theirs, weights, high, low, image,
                  lags, bins, high0, low0, high1, low1, state, sems):
    levels, kernels, freqs, grid, lag_count = dims
    depth, core = lax.axis_index("depth"), lax.axis_index("freq")
    freq, layer = lax.rem(depth, freqs), lax.div(depth, freqs)
    strip_index, group = lax.rem(layer, STRIPS), lax.div(layer, STRIPS)
    strip = grid // STRIPS
    span = TAPS * WIN
    counts = tile_counts(levels, grid)
    for piece, other in ((mine, core), (theirs, 1 - core)):
        for number in range(mine.shape[0]):
            turn = 1 + number + other * mine.shape[0]
            bins[lax.rem(depth - turn + 2 * levels, levels)] = piece[number]
    fetch(((lags_far, lags), (own.at[0], bins.at[depth])), sems)

    def descend(forward):
        def row_of(tile):
            return (tile if forward else grid // TILE - 1 - tile) * TILE

        def spread_between(there, number, before, after):
            planes = []
            for old, new in zip(before, after):
                halves = [old[EDGE:], new[:EDGE]] if forward else [new[EDGE:], old[:EDGE]]
                planes.append(jnp.concatenate(halves, axis=0))
            spread(*there, (number if forward else grid // TILE - number) * TILE, planes)

        def advance(high, low, level, row):
            cell_bins = bins[level, pl.ds(row, TILE), :]
            sums = []
            for which in range(3):
                rhs = high[which, :, pl.ds(row, WIN), :].reshape(span, 2 * LANES)
                rhs_low = low[which, :, pl.ds(row, WIN), :].reshape(span, 2 * LANES)
                out = jnp.dot(weights[which, :, : 3 * span], jnp.concatenate([rhs, rhs, rhs_low], axis=0), preferred_element_type=F32)
                for field in range(2):
                    chosen = jnp.zeros((TILE, LANES), F32)
                    for k in range(kernels):
                        chosen = jnp.where(cell_bins == k, out[k * TILE : (k + 1) * TILE, field * LANES : (field + 1) * LANES], chosen)
                    sums.append(chosen)
            planes = []
            for field in range(2):
                planes.append(sums[field] - sums[2 + field])
                planes.append(sums[field] + sums[4 + field])
            for plane in range(4):
                state[level % 2, plane, pl.ds(row, TILE), :] = planes[plane]
            return tuple(planes)

        def correlate(level):
            start = 0 if forward else grid - strip
            planes = [state[level % 2, plane, pl.ds(start, strip), :] for plane in range(4)]
            lanes = lax.broadcasted_iota(jnp.int32, (strip, LANES), 1)
            z, y = level // freqs, level % freqs
            place = (z % STRIPS ^ core) * freqs + (y ^ freq)
            place = jnp.where(group == z // STRIPS, place, STRIPS * freqs)
            for number in range(lag_count):
                offset = lags[number]
                away = lax.rem(LANES - offset, LANES)
                s_re, s_im = pltpu.roll(planes[0], offset, 1), pltpu.roll(planes[1], offset, 1)
                r_re, r_im = pltpu.roll(planes[2], away, 1), pltpu.roll(planes[3], away, 1)
                inside = (lanes >= offset) & (lanes < LANES - offset)
                image[place, pl.ds(number, strip, stride=lag_count), :] = jnp.where(inside, s_re * r_re + s_im * r_im, 0.0)

        slots = [(high, low), (high1, low1)] + [(high0, low0), (high1, low1)] * levels
        zeros = tuple(jnp.zeros((TILE, LANES), F32) for _ in range(4))
        before = after = zeros
        for level in range(levels):
            here, there = slots[level], slots[level + 1]
            first = advance(*here, level, row_of(0))
            if level:
                spread_between(here, counts[level - 1] - 1, before, after)
                if counts[level] == counts[level - 1]:
                    spread_between(here, counts[level], after, zeros)
                correlate(level - 1)
            before, after = zeros, first
            for number in range(1, counts[level]):
                fresh = advance(*here, level, row_of(number))
                if level < levels - 1:
                    spread_between(there, number - 1, before, after)
                before, after = after, fresh
        correlate(levels - 1)

    for number in range(STRIPS):

        @pl.when(strip_index == number)
        def _(number=number):
            descend(number == 0)


def run_levels(lags, surface, bins, stencil, step, shift, levels):
    freqs, _, grid, _ = surface.shape
    kernels = step.shape[1]
    rows = grid + 2 * EDGE
    dims = (levels, kernels, freqs, grid, lags.shape[0])
    span = -(-3 * TAPS * WIN // LANES)
    vm = pl.BlockSpec(memory_space=pltpu.VMEM)
    sm = pl.BlockSpec(memory_space=pltpu.SMEM)
    operand = (3, TAPS, rows, 2 * LANES)
    far = pl.BlockSpec(memory_space=pltpu.HBM)
    weights = pl.pallas_call(
        functools.partial(weights_kernel, dims),
        out_shape=jax.ShapeDtypeStruct((3, kernels * TILE, span * LANES), BF),
        in_specs=[far] * 3,
        out_specs=vm,
        scratch_shapes=[
            pltpu.VMEM((5, freqs, kernels), F32),
            pltpu.VMEM((freqs, kernels), F32),
            pltpu.VMEM((freqs, kernels), F32),
            pltpu.VMEM((span, kernels * TILE, LANES), F32),
            pltpu.SemaphoreType.DMA((3,)),
        ],
        compiler_params=pltpu.CompilerParams(vmem_limit_bytes=8 * 1024 * 1024),
    )(*map(distant, (jnp.transpose(stencil, (2, 0, 1)), step, shift)))
    high, low = pl.pallas_call(
        functools.partial(operands_kernel, dims),
        out_shape=[jax.ShapeDtypeStruct(operand, BF)] * 2,
        in_specs=[far],
        out_specs=[vm] * 2,
        scratch_shapes=[
            pltpu.VMEM((2, grid, 2 * grid), F32),
            pltpu.VMEM((4, rows, LANES), F32),
            pltpu.SemaphoreType.DMA((1,)),
        ],
        compiler_params=pltpu.CompilerParams(vmem_limit_bytes=12 * 1024 * 1024),
    )(distant(surface))
    received, weights, high, low = lax.optimization_barrier((fetch_bins(bins, STRIPS * freqs), weights, high, low))
    mine, theirs = swap_bins(received)
    return pl.pallas_call(
        functools.partial(levels_kernel, dims),
        out_shape=jax.ShapeDtypeStruct((STRIPS * freqs + 1, grid // STRIPS * lags.shape[0], grid), F32),
        in_specs=[far, far] + [vm] * 5,
        out_specs=vm,
        scratch_shapes=[pltpu.SMEM(lags.shape, jnp.int32), pltpu.VMEM((levels, grid, LANES), jnp.int32)]
        + [pltpu.VMEM(operand, BF)] * 4
        + [pltpu.VMEM((2, 4, grid, LANES), F32), pltpu.SemaphoreType.DMA((2,))],
        compiler_params=pltpu.CompilerParams(vmem_limit_bytes=32 * 1024 * 1024),
    )(distant(lags), distant(bins), mine, theirs, weights, high, low)


column_tile = 16


def from_behind(value, axis, steps):
    count = lax.axis_size(axis)
    initial, last = (max(0, -steps), min(count, count - steps))
    return lax.ppermute(value, axis, [(source, source + steps) for source in range(initial, last)])


def kernel_taps(stencil, phase_step, phase_shift):
    center = stencil[..., 0]
    along_x = stencil[..., 1]
    along_y = stencil[..., 2]
    diag_main = stencil[..., 3]
    diag_anti = stencil[..., 4]
    row_above = jnp.stack([diag_main, along_y, diag_anti], -1)
    row_middle = jnp.stack([along_x, center, along_x], -1)
    row_below = jnp.stack([diag_anti, along_y, diag_main], -1)
    stencil_grid = jnp.stack([row_above, row_middle, row_below], -2)
    weight_sum = center + 2.0 * (along_x + along_y + diag_main + diag_anti)
    stencil_grid = stencil_grid * (phase_step / weight_sum)[..., None, None]
    lead = stencil.shape[:-1]
    tap_rows = lax.broadcasted_iota(jnp.int32, (TAPS, TAPS), 0)
    tap_cols = lax.broadcasted_iota(jnp.int32, (TAPS, TAPS), 1)
    unit_tap = ((tap_rows == HALF) & (tap_cols == HALF)).astype(jnp.float32)
    power = jnp.broadcast_to(unit_tap, lead + (TAPS, TAPS))
    real_sum = power
    imag_sum = jnp.zeros(lead + (TAPS, TAPS), jnp.float32)
    pad_spec = [(0, 0)] * len(lead) + [(1, 1), (1, 1)]
    for order in range(1, HALF + 1):
        padded = jnp.pad(power, pad_spec)
        grown = jnp.zeros(lead + (TAPS, TAPS), jnp.float32)
        for row_off in range(3):
            for col_off in range(3):
                piece = padded[
                    ..., 2 - row_off : 2 - row_off + TAPS, 2 - col_off : 2 - col_off + TAPS
                ]
                grown = grown + stencil_grid[..., row_off, col_off, None, None] * piece
        power = grown
        weighted = power * (1.0 / math.factorial(order))
        if order % 4 == 1:
            imag_sum = imag_sum + weighted
        elif order % 4 == 2:
            real_sum = real_sum - weighted
        elif order % 4 == 3:
            imag_sum = imag_sum - weighted
        else:
            real_sum = real_sum + weighted
    cosine = jnp.cos(phase_shift)[..., None, None]
    sine = jnp.sin(phase_shift)[..., None, None]
    return (cosine * real_sum - sine * imag_sum, sine * real_sum + cosine * imag_sum)


def advance_level(fields, weights, selector):
    field_count = fields.shape[0]
    grid_width = fields.shape[1]
    tiles = grid_width // column_tile
    parts = fields.reshape(field_count, grid_width, 2, grid_width)
    padded = jnp.pad(parts, ((0, 0), (HALF, HALF), (0, 0), (HALF, column_tile - HALF)))
    main = padded[..., :grid_width].reshape(
        field_count, grid_width + 2 * HALF, 2, tiles, column_tile
    )
    after = padded[..., column_tile : grid_width + column_tile].reshape(
        field_count, grid_width + 2 * HALF, 2, tiles, column_tile
    )
    windows = jnp.concatenate([main, after[..., : 2 * HALF]], -1)
    windows = jnp.transpose(windows, (0, 1, 3, 2, 4))
    patches = jnp.stack(
        [windows[:, row_tap : row_tap + grid_width] for row_tap in range(TAPS)], axis=3
    )
    patches = patches.reshape(field_count * grid_width * tiles, TAPS * 2 * (column_tile + 2 * HALF))
    result = jnp.dot(
        patches, weights, precision=lax.Precision.HIGHEST, preferred_element_type=jnp.float32
    )
    result = result.reshape(field_count, grid_width, tiles, KERNELS, 2, column_tile)
    chosen = jnp.sum(result * selector[None], axis=3)
    return jnp.transpose(chosen, (0, 1, 3, 2, 4)).reshape(field_count, grid_width, 2 * grid_width)


def image_terms(source, receiver, lags):
    grid_width = source.shape[0]
    source_parts = jnp.pad(
        source.reshape(grid_width, 2, grid_width), ((0, 0), (0, 0), (HMAX, HMAX))
    )
    receiver_parts = jnp.pad(
        receiver.reshape(grid_width, 2, grid_width), ((0, 0), (0, 0), (HMAX, HMAX))
    )
    lag_terms = []
    for lag_index in range(LAGS):
        offset = lags[lag_index]
        shifted_source = lax.dynamic_slice_in_dim(source_parts, HMAX - offset, grid_width, 2)
        shifted_receiver = lax.dynamic_slice_in_dim(receiver_parts, HMAX + offset, grid_width, 2)
        lag_terms.append(jnp.sum(shifted_source * shifted_receiver, axis=1))
    return jnp.stack(lag_terms)


def pipeline_body(surface, bins, stencil, phase_step, phase_shift, lags):
    shot_count = surface.shape[0]
    freq_count = surface.shape[1]
    grid_width = surface.shape[3]
    slab_steps = bins.shape[0]
    tiles = grid_width // column_tile
    window_width = column_tile + 2 * HALF
    depth_count = lax.axis_size("depth")
    depth_index = lax.axis_index("depth")
    kern_real, kern_imag = kernel_taps(stencil, phase_step, phase_shift)
    mixing = jnp.stack(
        [jnp.stack([kern_real, kern_imag], 1), jnp.stack([-kern_imag, kern_real], 1)], 1
    )
    window_ids = lax.broadcasted_iota(jnp.int32, (window_width, column_tile, TAPS), 0)
    out_ids = lax.broadcasted_iota(jnp.int32, (window_width, column_tile, TAPS), 1)
    tap_ids = lax.broadcasted_iota(jnp.int32, (window_width, column_tile, TAPS), 2)
    shift_table = (window_ids == out_ids + tap_ids).astype(jnp.float32)
    all_weights = jnp.einsum(
        "fpqkab,cwb->fapckqw", mixing, shift_table, precision=lax.Precision.HIGHEST
    )
    all_weights = all_weights.reshape(
        freq_count, TAPS * 2 * window_width, KERNELS * 2 * column_tile
    )
    kernel_ids = lax.broadcasted_iota(jnp.int32, (1, 1, 1, KERNELS, 1, 1), 3)
    selectors = (
        bins.reshape(slab_steps, grid_width, tiles, 1, 1, column_tile) == kernel_ids
    ).astype(jnp.float32)
    image_part = jnp.zeros((slab_steps, LAGS, grid_width, grid_width), jnp.float32)
    front_count = shot_count * freq_count

    def advance_turn(step_index, carry):
        sent, image_now = carry
        received = from_behind(sent, "depth", 1)
        front_index = step_index - depth_index
        active = (front_index >= 0) & (front_index < front_count)
        clipped = jnp.clip(front_index, 0, front_count - 1)
        shot_index = clipped // freq_count
        freq_index = clipped % freq_count
        shot_fields = lax.dynamic_index_in_dim(surface, shot_index, 0, keepdims=False)
        surface_front = lax.dynamic_index_in_dim(shot_fields, freq_index, 0, keepdims=False)
        incoming = jnp.where(depth_index == 0, surface_front, received)
        weights_front = lax.dynamic_index_in_dim(all_weights, freq_index, 0, keepdims=False)

        def compute_front(state):
            fields, image_held = state
            fields = advance_level(fields, weights_front, selectors[0])
            level_terms = [image_terms(fields[0], fields[1], lags)]
            return (fields, image_held + jnp.stack(level_terms))

        def keep_state(state):
            return state

        return lax.cond(active, compute_front, keep_state, (incoming, image_now))

    start = (jnp.zeros((2, grid_width, 2 * grid_width), jnp.float32), image_part)
    final_sent, image_part = lax.fori_loop(0, depth_count + front_count - 1, advance_turn, start)
    image_part = image_part.reshape(slab_steps, LAGS, grid_width * grid_width)
    return lax.psum_scatter(image_part, "freq", scatter_dimension=2, tiled=True)


def fetch_bins(bins, group):
    count, cores = lax.axis_size("depth"), lax.axis_size("freq")
    rounds = -(-(count - 1) // cores)
    received = []
    for number in range(rounds):
        pairs = []
        for own in range(cores):
            turn = 1 + number + own * rounds
            for place in range(count if turn < count else 0):
                target = (place + turn) % count
                if target // group >= place // group:
                    pairs.append((place * cores + own, target * cores + own))
        received.append(lax.ppermute(bins[0], ("depth", "freq"), pairs))
    return received


def swap_bins(received):
    mine = jnp.stack(received)
    return mine, lax.ppermute(mine, "freq", [(0, 1), (1, 0)])


def spread_image(image, freqs, lags):
    count, cores = lax.axis_size("depth"), lax.axis_size("freq")
    grid = image.shape[2]
    block = image[:freqs] + lax.ppermute(image[freqs : 2 * freqs], "freq", [(0, 1), (1, 0)])
    total = None
    for turn in reversed(range(freqs)):
        pairs = []
        for depth in range(count):
            z, y = depth // freqs, depth % freqs
            for c in range(cores):
                target = (z // STRIPS * STRIPS + c) * freqs + (y ^ turn)
                pairs.append((depth * cores + c, target * cores + z % STRIPS))
        part = lax.ppermute(block[turn], ("depth", "freq"), pairs)
        total = part if total is None else total + part
    total = jnp.transpose(total.reshape(-1, lags, grid), (1, 0, 2))
    return total.reshape(1, lags, -1)


def strip_body(surface, bins, stencil, phase_step, phase_shift, lags):
    image = run_levels(lags, surface[0], bins, stencil, phase_step, phase_shift, lax.axis_size("depth"))
    return spread_image(image, surface.shape[1], lags.shape[0])


def body(surface, bins, stencil, phase_step, phase_shift, lags):
    count, cores = lax.axis_size("depth"), lax.axis_size("freq")
    freqs, grid = surface.shape[1], surface.shape[3]
    fits = (
        surface.shape[0] == 1
        and bins.shape[0] == 1
        and grid == LANES
        and cores == 2
        and freqs == 2
        and count % (STRIPS * freqs) == 0
        and count & (count - 1) == 0
        and HALF * (count - 1) <= grid // 2
    )
    way = strip_body if fits else pipeline_body
    return way(surface, bins, stencil, phase_step, phase_shift, lags)


def solution(mesh):
    return jax.shard_map(
        body,
        mesh=mesh,
        in_specs=(
            P("shots", "freq", None, None, None),
            P("depth", None, None),
            P("freq", None, None),
            P("freq", None),
            P("freq", None),
            P(),
        ),
        out_specs=P("depth", "shots", "freq"),
        check_vma=False,
    )
```
